512 devices in a mesh: lat: 16 (over x_hi, y), lon: 32 (over z, x_lo, core).
Axes of the slice: x: 4 (x_hi: 2, x_lo: 2; x = x_hi * 2 + x_lo), y: 8, z: 8, core: 2. Of those that a mesh axis runs over, the one named last changes fastest.
Arguments:
- height: float32 [1024, 8640], P('lat', 'lon'), may hold values from -6 to 6
- east_flow: float32 [1024, 8640], P('lat', 'lon'), may hold values from -4 to 4
- north_flow: float32 [1024, 8640], P('lat', 'lon'), may hold values from -4 to 4
- legendre: float32 [128, 1024, 2048], P('lon', 'lat'), may hold values from -0.1875 to 0.1875
- love_numbers: float32 [2048], replicated, may hold values from 0.05 to 1
- wavenumbers: int32 [128], replicated, may hold values from 0 to 2047, as said below
- land_sea: int32 [1024, 8640], P('lat', 'lon'), may hold values 0 or 1
Outputs:
- loading: float32 [1024, 8640], P('lat', 'lon')
- surface: float32 [1024, 8640], P('lat', 'lon')
- east_out: float32 [1024, 8640], P('lat', 'lon')
- north_out: float32 [1024, 8640], P('lat', 'lon')
The draws below stay inside these ranges and needn't reach their ends.
Inputs may be any that keep to these rules, and one draw needn't show every extreme that they name: 128 distinct wavenumbers in no particular order; 0 and 2047 are always among them.
All inputs are finite; a program needn't handle non-finite values. No bound on the sum of `land_sea` on one device may be relied on, other than what follows from the above.
Results may differ from the reference program's by a relative error of at most 0.000078.
Values sent between devices are 32-bit elements; how exact they have to be, the bound alone decides.
A program may use at most 64 MiB of HBM per device.

```python
import math
import jax
import jax.numpy as jnp
from jax import lax

NLON = 8640
DEGREES = 2048
KMAX = 2048
SUBSTEPS = 4
WAVES = 128
NLAT = 1024


def draw_wavenumbers(key, part):
    chosen = jax.random.permutation(key, KMAX - 2)[:WAVES - 2] + 1
    ends = jnp.array([0, KMAX - 1], dtype=jnp.int32)
    mixed = jnp.concatenate([chosen.astype(jnp.int32), ends])
    return jax.random.permutation(jax.random.fold_in(key, 7), mixed).astype(jnp.int32)


def set_ends(entries, stream_key, low, largest):
    place = [jax.random.randint(jax.random.fold_in(stream_key, axis), (), 0, length) for axis, length in enumerate(entries.shape)]
    widest = entries.shape.index(max(entries.shape))
    beside = place[:widest] + [(place[widest] + 1) % entries.shape[widest]] + place[widest + 1:]
    return entries.at[tuple(place)].set(low).at[tuple(beside)].set(largest)


def block_levels(rng, extent, cuts, low, largest):
    gain = 1.0
    for axis_at, blocks in cuts:
        heights = jax.random.uniform(jax.random.fold_in(jax.random.fold_in(rng, 6), axis_at), (blocks,), jnp.float32, low / len(cuts), largest / len(cuts))
        gain = gain * jnp.repeat(jnp.exp(heights), extent[axis_at] // blocks).reshape((-1,) + (1,) * (len(extent) - 1 - axis_at))
    return gain


def noise(key, dims, width, bound, cuts=(), kind=jnp.bfloat16):
    values = jax.random.normal(key, dims, jnp.float32) * width
    if len(cuts) > 0:
        values = block_levels(key, dims, cuts, -0.22, 0.18) * values
    return jnp.clip(values, min=-bound, max=bound).astype(kind)


def setup_inputs(seed: int = 0) -> dict:
    splits = jax.random.split(jax.random.key(seed), 8)
    return {
        "height": noise(splits[0], (NLAT, NLON), 1.0, 6.0, ((0, 16), (1, 32)), jnp.float32),
        "east_flow": noise(splits[1], (NLAT, NLON), 0.5, 4.0, ((0, 16), (1, 32)), jnp.float32),
        "north_flow": noise(splits[2], (NLAT, NLON), 0.5, 4.0, ((0, 16), (1, 32)), jnp.float32),
        "legendre": noise(splits[3], (WAVES, NLAT, DEGREES), NLAT ** -0.5, 0.1875, ((0, 32), (1, 16)), jnp.float32),
        "love_numbers": jnp.clip(jnp.exp(jax.random.uniform(splits[4], (DEGREES,), jnp.float32, math.log(0.05), math.log(1.0))), 0.05, 1.0),
        "wavenumbers": draw_wavenumbers(jax.random.fold_in(splits[7], 71), 0),
        "land_sea": set_ends((jax.random.randint(splits[6], (NLAT, NLON), 0, 5) < 4).astype(jnp.int32), jax.random.fold_in(splits[6], 1), 0, 1),
    }


def harmonic_rows(wavenumbers, first_column, column_count, period):
    columns = first_column + jnp.arange(column_count, dtype=jnp.int32)
    product = wavenumbers.astype(jnp.int32)[:, None] * columns[None, :] % period
    angles = 2.0 * math.pi / period * product.astype(jnp.float32)
    stacked = jnp.stack([jnp.cos(angles), jnp.sin(angles)], axis=1)
    return stacked.reshape(2 * wavenumbers.shape[0], column_count)

def reference(height, east_flow, north_flow, legendre, love_numbers, wavenumbers, land_sea):
    hp = lax.Precision.HIGHEST
    harmonics = harmonic_rows(wavenumbers, 0, NLON, NLON)
    fourier = lax.dot_general(harmonics, height, (((1,), (1,)), ((), ())), precision=hp) * (1.0 / math.sqrt(NLON))
    fourier = fourier.reshape(WAVES, 2, NLAT)
    spectral = jnp.einsum('mtl,mpt->mpl', legendre, fourier, precision=hp) * love_numbers[None, None, :]
    synthesized = jnp.einsum('mtl,mpl->mpt', legendre, spectral, precision=hp).reshape(2 * WAVES, NLAT)
    loading = lax.dot_general(synthesized, harmonics, (((0,), (0,)), ((), ())), precision=hp) * (1.0 / math.sqrt(WAVES))
    wet_cells = land_sea.astype(jnp.float32)
    surface = height
    east_out = east_flow
    north_out = north_flow
    for substep in range(SUBSTEPS):
        pressure = surface - loading
        padded = jnp.pad(pressure, ((1, 1), (0, 0)))
        east_out = wet_cells * (east_out - 0.3 * (jnp.roll(pressure, -1, 1) - jnp.roll(pressure, 1, 1)))
        north_out = wet_cells * (north_out - 0.3 * (padded[2:] - padded[:-2]))
        north_pad = jnp.pad(north_out, ((1, 1), (0, 0)))
        change = 0.3 * (jnp.roll(east_out, -1, 1) - jnp.roll(east_out, 1, 1)) + 0.3 * (north_pad[2:] - north_pad[:-2])
        surface = surface - wet_cells * change
    return (loading, surface, east_out, north_out)
```

```python
import functools
import math

import jax
import jax.numpy as jnp
from jax import lax
from jax.experimental import pallas as pl
from jax.experimental.pallas import tpu as pltpu
from jax.sharding import PartitionSpec as P

SUBSTEPS = 4
HALO = 2 * SUBSTEPS
LANES = 128
EAST_STEP = 0.3
NORTH_STEP = 0.3
MESH = pl.DeviceIdType.MESH
HIGHEST = lax.Precision.HIGHEST


def dot(a, b, dims):
    return lax.dot_general(
        a, b, (dims, ((), ())), precision=HIGHEST, preferred_element_type=jnp.float32
    )


def ring_order(n):
    return sorted(range(n), key=lambda d: -min(d, n - d))


def lat_partners(n_lat, lat):
    n_y = min(8, n_lat)
    x_hi, y = lat // n_y, lat % n_y
    steps = [(dx, dy) for dx in range(n_lat // n_y) for dy in range(n_y) if dx or dy]
    steps.sort(key=lambda s: -(2 * s[0] + min(s[1], n_y - s[1])))
    n_x = n_lat // n_y
    return [((x_hi + dx) % n_x) * n_y + (y + dy) % n_y for dx, dy in steps]


def lon_partners(n_lon, lon):
    n_z = n_lon // 4
    z, low = lon // 4, lon % 4
    steps = [(dz, e) for dz in ring_order(n_z) for e in (2, 3, 1, 0) if dz or e]
    return [((z + dz) % n_z) * 4 + (low + e) % 4 for dz, e in steps]


def kernel(
    n_lat,
    n_lon,
    height_ref,
    east_ref,
    north_ref,
    land_ref,
    legendre_ref,
    love_ref,
    waves_ref,
    loading_out,
    surface_out,
    east_out_ref,
    north_out_ref,
    fields,
    harmonics,
    twice,
    leg_own,
    leg_halo,
    a_out,
    a_in,
    b_out,
    b_in,
    c_out,
    c_in,
    d_out,
    d_in,
    to_left,
    to_right,
    from_right,
    from_left,
    leg_sem,
    send_sem,
    recv_sem,
    edge_send,
    edge_recv,
):
    lat = lax.axis_index("lat")
    lon = lax.axis_index("lon")
    rows, cols = height_ref.shape
    own = legendre_ref.shape[0]
    width = fields.shape[2]
    period = cols * n_lon
    base, rest = cols // LANES * LANES, cols % LANES
    lats = lat_partners(n_lat, lat)
    lons = lon_partners(n_lon, lon)

    barrier = pltpu.get_barrier_semaphore()
    for other in lons:
        pl.semaphore_signal(barrier, inc=1, device_id=(lat, other), device_id_type=MESH)
    for other in lats:
        pl.semaphore_signal(barrier, inc=1, device_id=(other, lon), device_id_type=MESH)
    leg_copy = pltpu.make_async_copy(legendre_ref, leg_own, leg_sem)
    leg_copy.start()

    for f, ref in enumerate((height_ref, east_ref, north_ref, land_ref)):
        fields[f, 0:rows, base:width] = jnp.zeros((rows, width - base), jnp.float32)
        fields[f, 0:rows, 0:cols] = ref[...].astype(jnp.float32)
    twice[0:rows, :] = fields[0, 0:rows, :]
    twice[rows : 2 * rows, :] = fields[0, 0:rows, :]

    count = waves_ref.shape[1]
    waves = jnp.broadcast_to(waves_ref[...].astype(jnp.float32), (LANES, count)).T
    start = jnp.bitwise_and(waves.astype(jnp.int32) * lon, n_lon - 1).astype(jnp.float32) * cols
    quarter = period // 4
    lane = lax.broadcasted_iota(jnp.int32, (8, width), 1)
    column = jnp.where(lane < width - 64, lane, lane - width).astype(jnp.float32)
    upper = lax.broadcasted_iota(jnp.int32, (8, width), 0) < 4
    for g in range(count // 8):
        wave = jnp.concatenate([waves[8 * g : 8 * g + 8]] * (width // LANES), axis=1)
        first = jnp.concatenate([start[8 * g : 8 * g + 8]] * (width // LANES), axis=1)
        r = wave * column + first
        turn = (r * (1.0 / quarter) + 4096.5).astype(jnp.int32)
        d = r - (turn - 4096).astype(jnp.float32) * quarter
        phi = d * (2.0 * math.pi / period)
        s = phi * phi
        sin = 1.0 / 362880.0
        sin = sin * s - 1.0 / 5040.0
        sin = sin * s + 1.0 / 120.0
        sin = sin * s - 1.0 / 6.0
        sin = phi + phi * (s * sin)
        cos = -1.0 / 3628800.0
        cos = cos * s + 1.0 / 40320.0
        cos = cos * s - 1.0 / 720.0
        cos = cos * s + 1.0 / 24.0
        cos = cos * s - 0.5
        cos = 1.0 + s * cos
        odd = jnp.bitwise_and(turn, 1) == 1
        cos_minus = jnp.bitwise_and(turn + 1, 2) == 2
        sin_minus = jnp.bitwise_and(turn, 2) == 2
        c = jnp.where(odd, sin, cos)
        c = jnp.where(cos_minus, -c, c)
        n = jnp.where(odd, cos, sin)
        n = jnp.where(sin_minus, -n, n)
        harmonics[16 * g : 16 * g + 8, :] = jnp.where(upper, c, pltpu.roll(n, 4, 0))
        harmonics[16 * g + 8 : 16 * g + 16, :] = jnp.where(upper, pltpu.roll(c, 4, 0), n)

    partial = dot(harmonics[...], twice[...], ((1,), (1,))) * (1.0 / math.sqrt(period))
    half = lax.broadcasted_iota(jnp.int32, (8, LANES), 1) < rows
    for j in range(n_lon):
        block = partial[8 * j : 8 * j + 8]
        a_out[j] = jnp.where(half, block, pltpu.roll(block, 4, 0))[0:4]

    pl.semaphore_wait(barrier, n_lat + n_lon - 2)

    def lon_copy(k, src, dst, other):
        return pltpu.make_async_remote_copy(
            src_ref=src,
            dst_ref=dst,
            send_sem=send_sem.at[k],
            recv_sem=recv_sem.at[k],
            device_id=(lat, other),
            device_id_type=MESH,
        )

    def lat_copy(k, src, dst, other):
        return pltpu.make_async_remote_copy(
            src_ref=src,
            dst_ref=dst,
            send_sem=send_sem.at[k],
            recv_sem=recv_sem.at[k],
            device_id=(other, lon),
            device_id_type=MESH,
        )

    def all_received(k, ref, n):
        pltpu.make_async_copy(ref.at[pl.ds(0, n)], ref.at[pl.ds(0, n)], recv_sem.at[k]).wait()

    def all_sent(k, ref, n):
        pltpu.make_async_copy(ref.at[pl.ds(0, n)], ref.at[pl.ds(0, n)], send_sem.at[k]).wait()

    for other in lons:
        lon_copy(0, a_out.at[other], a_in.at[lon], other).start()
    a_in[lon] = a_out[lon]

    below, above = jnp.minimum(lat + 1, n_lat - 1), jnp.maximum(lat - 1, 0)

    def edge_copy(k, src, dst, where):
        return pltpu.make_async_remote_copy(
            src_ref=src,
            dst_ref=dst,
            send_sem=edge_send.at[k],
            recv_sem=edge_recv.at[k],
            device_id=where,
            device_id_type=MESH,
        )

    low_rows = edge_copy(
        0, fields.at[:, 0:HALO, :], fields.at[:, rows : rows + HALO, :], (above, lon)
    )
    high_rows = edge_copy(
        1,
        fields.at[:, rows - HALO : rows, :],
        fields.at[:, rows + HALO : rows + 2 * HALO, :],
        (below, lon),
    )
    low_leg = edge_copy(
        2, legendre_ref.at[:, 0:HALO, :], leg_halo.at[:, 0:HALO, :], (above, lon)
    )
    high_leg = edge_copy(
        3,
        legendre_ref.at[:, rows - HALO : rows, :],
        leg_halo.at[:, HALO : 2 * HALO, :],
        (below, lon),
    )

    @pl.when(lat > 0)
    def _():
        low_rows.start()
        low_leg.start()

    @pl.when(lat < n_lat - 1)
    def _():
        high_rows.start()
        high_leg.start()

    @pl.when(lat == 0)
    def _():
        fields[:, rows + HALO : rows + 2 * HALO, :] = jnp.zeros((4, HALO, width), jnp.float32)
        leg_halo[:, HALO : 2 * HALO, :] = jnp.zeros((own, HALO, leg_halo.shape[2]), jnp.float32)

    @pl.when(lat == n_lat - 1)
    def _():
        fields[:, rows : rows + HALO, :] = jnp.zeros((4, HALO, width), jnp.float32)
        leg_halo[:, 0:HALO, :] = jnp.zeros((own, HALO, leg_halo.shape[2]), jnp.float32)

    leg_copy.wait()
    all_received(0, a_in, n_lon - 1)
    fourier = jnp.sum(a_in[...], axis=0)

    degrees = leg_own.shape[2]
    lane8 = lax.broadcasted_iota(jnp.int32, (8, LANES), 1)
    row8 = lax.broadcasted_iota(jnp.int32, (8, LANES), 0)
    both = jnp.concatenate([fourier, fourier], axis=0)
    swapped = pltpu.roll(both, rows, 1)
    spread = jnp.where((lane8 < rows) == (row8 < 4), both, swapped)
    wave8 = jnp.bitwise_and(row8, 3)
    left = jnp.concatenate(
        [jnp.where(wave8 == 2 * h + lane8 // rows, spread, 0.0) for h in range(own * rows // LANES)],
        axis=1,
    )
    part = dot(left, leg_own[...].reshape(own * rows, degrees), ((1,), (0,)))
    for i in range(n_lat):
        b_out[i] = part[:, LANES * i : LANES * (i + 1)]
    for other in lats:
        lat_copy(1, b_out.at[other], b_in.at[lat], other).start()
    b_in[lat] = b_out[lat]

    @pl.when(lat > 0)
    def _():
        high_rows.wait_recv()

    @pl.when(lat < n_lat - 1)
    def _():
        low_rows.wait_recv()

    deep = fields.shape[1]
    lane80 = lax.broadcasted_iota(jnp.int32, (deep, LANES), 1)
    packed_left = jnp.zeros((deep, LANES), jnp.float32)
    packed_right = jnp.zeros((deep, LANES), jnp.float32)
    for f in range(4):
        here = (lane80 >= 16 * f) & (lane80 < 16 * f + HALO)
        west = fields[f, :, 0:LANES]
        east = fields[f, :, base : base + LANES]
        packed_left = jnp.where(here, pltpu.roll(west, 16 * f, 1), packed_left)
        packed_right = jnp.where(
            here, pltpu.roll(east, (16 * f - (rest - HALO)) % LANES, 1), packed_right
        )
    to_left[...] = packed_left
    to_right[...] = packed_right
    west_side, east_side = lax.rem(lon + n_lon - 1, n_lon), lax.rem(lon + 1, n_lon)
    left_copy = edge_copy(4, to_left, from_right, (lat, west_side))
    right_copy = edge_copy(5, to_right, from_left, (lat, east_side))
    left_copy.start()
    right_copy.start()

    all_received(1, b_in, n_lat - 1)

    c_out[...] = jnp.sum(b_in[...], axis=0)
    for other in lats:
        lat_copy(2, c_out, c_in.at[lat], other).start()
    c_in[lat] = c_out[...]

    @pl.when(lat > 0)
    def _():
        low_rows.wait_send()

    @pl.when(lat < n_lat - 1)
    def _():
        high_rows.wait_send()

    left_copy.wait_recv()
    right_copy.wait_recv()
    right_halo = from_right[...]
    left_halo = from_left[...]
    for f in range(4):
        tile = fields[f, :, base : base + LANES]
        tile = jnp.where(
            (lane80 >= rest) & (lane80 < rest + HALO),
            pltpu.roll(right_halo, (rest - 16 * f) % LANES, 1),
            tile,
        )
        tile = jnp.where(
            lane80 >= LANES - HALO,
            pltpu.roll(left_halo, (LANES - HALO - 16 * f) % LANES, 1),
            tile,
        )
        fields[f, :, base : base + LANES] = tile

    @pl.when(lat > 0)
    def _():
        high_leg.wait_recv()

    @pl.when(lat < n_lat - 1)
    def _():
        low_leg.wait_recv()

    all_received(2, c_in, n_lat - 1)

    spectral = jnp.concatenate([c_in[i] for i in range(n_lat)], axis=1) * love_ref[...]
    inner = dot(spectral, leg_own[...].reshape(own * rows, degrees), ((1,), (1,)))
    outer = dot(spectral, leg_halo[...].reshape(own * 2 * HALO, degrees), ((1,), (1,)))
    body = jnp.zeros((8, LANES), jnp.float32)
    for h in range(own * rows // LANES):
        body = body + jnp.where(
            wave8 == 2 * h + lane8 // rows, inner[:, LANES * h : LANES * (h + 1)], 0.0
        )
    body = body + pltpu.roll(body, rows, 1)
    rim = jnp.concatenate(
        [outer, jnp.zeros((8, LANES - own * 2 * HALO), jnp.float32)], axis=1
    )
    rim = jnp.where(wave8 == lane8 // (2 * HALO), rim, 0.0)
    folded = pltpu.roll(rim, rows, 1)
    for m in range(1, own):
        folded = folded + pltpu.roll(rim, rows - 2 * HALO * m, 1)
    synthesized = jnp.where(
        lane8 < rows, body, jnp.where(lane8 < rows + 2 * HALO, folded, 0.0)
    )
    d_out[...] = synthesized * (1.0 / math.sqrt(count))
    for other in lons:
        lon_copy(3, d_out, d_in.at[lon], other).start()
    d_in[lon] = d_out[...]
    all_received(3, d_in, n_lon - 1)

    loading = dot(d_in[...].reshape(8 * n_lon, LANES), harmonics[...], ((0,), (0,)))[0:deep]

    surface = fields[0]
    east = fields[1]
    north = fields[2]
    wet = fields[3]
    wide, tall = width - 1, deep - 1
    for _ in range(SUBSTEPS):
        pressure = surface - loading
        east = wet * (
            east - EAST_STEP * (pltpu.roll(pressure, wide, 1) - pltpu.roll(pressure, 1, 1))
        )
        north = wet * (
            north - NORTH_STEP * (pltpu.roll(pressure, tall, 0) - pltpu.roll(pressure, 1, 0))
        )
        change = EAST_STEP * (pltpu.roll(east, wide, 1) - pltpu.roll(east, 1, 1)) + NORTH_STEP * (
            pltpu.roll(north, tall, 0) - pltpu.roll(north, 1, 0)
        )
        surface = surface - wet * change
    loading_out[...] = loading[0:rows, 0:cols]
    surface_out[...] = surface[0:rows, 0:cols]
    east_out_ref[...] = east[0:rows, 0:cols]
    north_out_ref[...] = north[0:rows, 0:cols]

    all_sent(0, a_in, n_lon - 1)
    all_sent(1, b_in, n_lat - 1)
    all_sent(2, c_in, n_lat - 1)
    all_sent(3, d_in, n_lon - 1)
    left_copy.wait_send()
    right_copy.wait_send()

    @pl.when(lat > 0)
    def _():
        low_leg.wait_send()

    @pl.when(lat < n_lat - 1)
    def _():
        high_leg.wait_send()


def shards(height, east_flow, north_flow, legendre, love_numbers, wavenumbers, land_sea):
    n_lat, n_lon = lax.axis_size("lat"), lax.axis_size("lon")
    rows, cols = height.shape
    own, _, degrees = legendre.shape
    width = -(-(cols + 2 * HALO) // LANES) * LANES
    deep = rows + 2 * HALO
    vmem = pl.BlockSpec(memory_space=pltpu.VMEM)
    f32 = jnp.float32
    shape = jax.ShapeDtypeStruct((rows, cols), f32)
    return pl.pallas_call(
        functools.partial(kernel, n_lat, n_lon),
        out_shape=(shape, shape, shape, shape),
        in_specs=[vmem, vmem, vmem, vmem, pl.BlockSpec(memory_space=pl.ANY), vmem, vmem],
        out_specs=(vmem, vmem, vmem, vmem),
        scratch_shapes=[
            pltpu.VMEM((4, deep, width), f32),
            pltpu.VMEM((8 * n_lon, width), f32),
            pltpu.VMEM((2 * rows, width), f32),
            pltpu.VMEM((own, rows, degrees), f32),
            pltpu.VMEM((own, 2 * HALO, degrees), f32),
            pltpu.VMEM((n_lon, own, LANES), f32),
            pltpu.VMEM((n_lon, own, LANES), f32),
            pltpu.VMEM((n_lat, 8, LANES), f32),
            pltpu.VMEM((n_lat, 8, LANES), f32),
            pltpu.VMEM((8, LANES), f32),
            pltpu.VMEM((n_lat, 8, LANES), f32),
            pltpu.VMEM((8, LANES), f32),
            pltpu.VMEM((n_lon, 8, LANES), f32),
            pltpu.VMEM((deep, LANES), f32),
            pltpu.VMEM((deep, LANES), f32),
            pltpu.VMEM((deep, LANES), f32),
            pltpu.VMEM((deep, LANES), f32),
            pltpu.SemaphoreType.DMA,
            pltpu.SemaphoreType.DMA((4,)),
            pltpu.SemaphoreType.DMA((4,)),
            pltpu.SemaphoreType.DMA((6,)),
            pltpu.SemaphoreType.DMA((6,)),
        ],
        compiler_params=pltpu.CompilerParams(collective_id=0, has_side_effects=True),
    )(
        height,
        east_flow,
        north_flow,
        land_sea,
        legendre,
        love_numbers.reshape(1, degrees),
        wavenumbers.reshape(1, wavenumbers.shape[0]),
    )


def solution(mesh):
    return jax.shard_map(
        shards,
        mesh=mesh,
        in_specs=(
            P("lat", "lon"),
            P("lat", "lon"),
            P("lat", "lon"),
            P("lon", "lat", None),
            P(),
            P(),
            P("lat", "lon"),
        ),
        out_specs=(P("lat", "lon"), P("lat", "lon"), P("lat", "lon"), P("lat", "lon")),
        check_vma=False,
    )
```

```python
import functools
import math

import jax
import jax.numpy as jnp
from jax import lax
from jax.experimental import pallas as pl
from jax.experimental.pallas import tpu as pltpu
from jax.sharding import PartitionSpec as P

SUBSTEPS = 4
HALO = 2 * SUBSTEPS
LANES = 128
EAST_STEP = 0.3
NORTH_STEP = 0.3
MESH = pl.DeviceIdType.MESH
HIGHEST = lax.Precision.HIGHEST


def dot(a, b, dims):
    return lax.dot_general(
        a, b, (dims, ((), ())), precision=HIGHEST, preferred_element_type=jnp.float32
    )


def ring_order(n):
    return sorted(range(n), key=lambda d: -min(d, n - d))


def lat_partners(n_lat, lat):
    n_y = min(8, n_lat)
    x_hi, y = lat // n_y, lat % n_y
    steps = [(dx, dy) for dx in range(n_lat // n_y) for dy in range(n_y) if dx or dy]
    steps.sort(key=lambda s: -(2 * s[0] + min(s[1], n_y - s[1])))
    n_x = n_lat // n_y
    return [((x_hi + dx) % n_x) * n_y + (y + dy) % n_y for dx, dy in steps]


def lon_partners(n_lon, lon):
    n_z = n_lon // 4
    z, low = lon // 4, lon % 4
    steps = [(dz, e) for dz in ring_order(n_z) for e in (2, 3, 1, 0) if dz or e]
    return [((z + dz) % n_z) * 4 + (low + e) % 4 for dz, e in steps]


def kernel(
    n_lat,
    n_lon,
    height_hbm,
    east_hbm,
    north_hbm,
    land_hbm,
    legendre_ref,
    love_hbm,
    waves_hbm,
    loading_out,
    surface_out,
    east_out_ref,
    north_out_ref,
    height_ref,
    east_ref,
    north_ref,
    land_ref,
    love_ref,
    waves_ref,
    fields,
    harmonics,
    twice,
    leg_own,
    leg_halo,
    a_out,
    a_in,
    b_out,
    b_in,
    c_out,
    c_in,
    d_out,
    d_in,
    to_left,
    to_right,
    from_right,
    from_left,
    in_sem,
    send_sem,
    recv_sem,
    edge_send,
    edge_recv,
):
    lat = lax.axis_index("lat")
    lon = lax.axis_index("lon")
    rows, cols = height_ref.shape
    own = legendre_ref.shape[0]
    width = fields.shape[2]
    period = cols * n_lon
    base, rest = cols // LANES * LANES, cols % LANES
    lats = lat_partners(n_lat, lat)
    lons = lon_partners(n_lon, lon)

    inputs = [
        pltpu.make_async_copy(src, dst, in_sem.at[k])
        for k, (src, dst) in enumerate(
            (
                (waves_hbm, waves_ref),
                (height_hbm, height_ref),
                (east_hbm, east_ref),
                (north_hbm, north_ref),
                (land_hbm, land_ref),
                (love_hbm, love_ref),
                (legendre_ref, leg_own),
            )
        )
    ]
    for copy in inputs:
        copy.start()
    barrier = pltpu.get_barrier_semaphore()
    for other in lons:
        pl.semaphore_signal(barrier, inc=1, device_id=(lat, other), device_id_type=MESH)
    for other in lats:
        pl.semaphore_signal(barrier, inc=1, device_id=(other, lon), device_id_type=MESH)
    for copy in inputs[:6]:
        copy.wait()

    for f, ref in enumerate((height_ref, east_ref, north_ref, land_ref)):
        fields[f, 0:rows, base:width] = jnp.zeros((rows, width - base), jnp.float32)
        fields[f, 0:rows, 0:cols] = ref[...].astype(jnp.float32)
    twice[0:rows, :] = fields[0, 0:rows, :]
    twice[rows : 2 * rows, :] = fields[0, 0:rows, :]

    count = waves_ref.shape[1]
    waves = jnp.broadcast_to(waves_ref[...].astype(jnp.float32), (LANES, count)).T
    start = jnp.bitwise_and(waves.astype(jnp.int32) * lon, n_lon - 1).astype(jnp.float32) * cols
    quarter = period // 4
    lane = lax.broadcasted_iota(jnp.int32, (8, width), 1)
    column = jnp.where(lane < width - 64, lane, lane - width).astype(jnp.float32)
    upper = lax.broadcasted_iota(jnp.int32, (8, width), 0) < 4
    for g in range(count // 8):
        wave = jnp.concatenate([waves[8 * g : 8 * g + 8]] * (width // LANES), axis=1)
        first = jnp.concatenate([start[8 * g : 8 * g + 8]] * (width // LANES), axis=1)
        r = wave * column + first
        turn = (r * (1.0 / quarter) + 4096.5).astype(jnp.int32)
        d = r - (turn - 4096).astype(jnp.float32) * quarter
        phi = d * (2.0 * math.pi / period)
        s = phi * phi
        sin = 1.0 / 362880.0
        sin = sin * s - 1.0 / 5040.0
        sin = sin * s + 1.0 / 120.0
        sin = sin * s - 1.0 / 6.0
        sin = phi + phi * (s * sin)
        cos = -1.0 / 3628800.0
        cos = cos * s + 1.0 / 40320.0
        cos = cos * s - 1.0 / 720.0
        cos = cos * s + 1.0 / 24.0
        cos = cos * s - 0.5
        cos = 1.0 + s * cos
        odd = jnp.bitwise_and(turn, 1) == 1
        cos_minus = jnp.bitwise_and(turn + 1, 2) == 2
        sin_minus = jnp.bitwise_and(turn, 2) == 2
        c = jnp.where(odd, sin, cos)
        c = jnp.where(cos_minus, -c, c)
        n = jnp.where(odd, cos, sin)
        n = jnp.where(sin_minus, -n, n)
        harmonics[16 * g : 16 * g + 8, :] = jnp.where(upper, c, pltpu.roll(n, 4, 0))
        harmonics[16 * g + 8 : 16 * g + 16, :] = jnp.where(upper, pltpu.roll(c, 4, 0), n)

    partial = dot(harmonics[...], twice[...], ((1,), (1,))) * (1.0 / math.sqrt(period))
    half = lax.broadcasted_iota(jnp.int32, (8, LANES), 1) < rows
    for j in range(n_lon):
        block = partial[8 * j : 8 * j + 8]
        a_out[j] = jnp.where(half, block, pltpu.roll(block, 4, 0))[0:4]

    pl.semaphore_wait(barrier, n_lat + n_lon - 2)

    def lon_copy(k, src, dst, other):
        return pltpu.make_async_remote_copy(
            src_ref=src,
            dst_ref=dst,
            send_sem=send_sem.at[k],
            recv_sem=recv_sem.at[k],
            device_id=(lat, other),
            device_id_type=MESH,
        )

    def lat_copy(k, src, dst, other):
        return pltpu.make_async_remote_copy(
            src_ref=src,
            dst_ref=dst,
            send_sem=send_sem.at[k],
            recv_sem=recv_sem.at[k],
            device_id=(other, lon),
            device_id_type=MESH,
        )

    def all_received(k, ref, n):
        pltpu.make_async_copy(ref.at[pl.ds(0, n)], ref.at[pl.ds(0, n)], recv_sem.at[k]).wait()

    def all_sent(k, ref, n):
        pltpu.make_async_copy(ref.at[pl.ds(0, n)], ref.at[pl.ds(0, n)], send_sem.at[k]).wait()

    for other in lons:
        lon_copy(0, a_out.at[other], a_in.at[lon], other).start()
    a_in[lon] = a_out[lon]

    below, above = jnp.minimum(lat + 1, n_lat - 1), jnp.maximum(lat - 1, 0)

    def edge_copy(k, src, dst, where):
        return pltpu.make_async_remote_copy(
            src_ref=src,
            dst_ref=dst,
            send_sem=edge_send.at[k],
            recv_sem=edge_recv.at[k],
            device_id=where,
            device_id_type=MESH,
        )

    low_rows = edge_copy(
        0, fields.at[:, 0:HALO, :], fields.at[:, rows : rows + HALO, :], (above, lon)
    )
    high_rows = edge_copy(
        1,
        fields.at[:, rows - HALO : rows, :],
        fields.at[:, rows + HALO : rows + 2 * HALO, :],
        (below, lon),
    )
    low_leg = edge_copy(
        2, legendre_ref.at[:, 0:HALO, :], leg_halo.at[:, 0:HALO, :], (above, lon)
    )
    high_leg = edge_copy(
        3,
        legendre_ref.at[:, rows - HALO : rows, :],
        leg_halo.at[:, HALO : 2 * HALO, :],
        (below, lon),
    )

    @pl.when(lat > 0)
    def _():
        low_rows.start()
        low_leg.start()

    @pl.when(lat < n_lat - 1)
    def _():
        high_rows.start()
        high_leg.start()

    @pl.when(lat == 0)
    def _():
        fields[:, rows + HALO : rows + 2 * HALO, :] = jnp.zeros((4, HALO, width), jnp.float32)
        leg_halo[:, HALO : 2 * HALO, :] = jnp.zeros((own, HALO, leg_halo.shape[2]), jnp.float32)

    @pl.when(lat == n_lat - 1)
    def _():
        fields[:, rows : rows + HALO, :] = jnp.zeros((4, HALO, width), jnp.float32)
        leg_halo[:, 0:HALO, :] = jnp.zeros((own, HALO, leg_halo.shape[2]), jnp.float32)

    inputs[6].wait()
    all_received(0, a_in, n_lon - 1)
    fourier = jnp.sum(a_in[...], axis=0)

    degrees = leg_own.shape[2]
    lane8 = lax.broadcasted_iota(jnp.int32, (8, LANES), 1)
    row8 = lax.broadcasted_iota(jnp.int32, (8, LANES), 0)
    both = jnp.concatenate([fourier, fourier], axis=0)
    swapped = pltpu.roll(both, rows, 1)
    spread = jnp.where((lane8 < rows) == (row8 < 4), both, swapped)
    wave8 = jnp.bitwise_and(row8, 3)
    left = jnp.concatenate(
        [jnp.where(wave8 == 2 * h + lane8 // rows, spread, 0.0) for h in range(own * rows // LANES)],
        axis=1,
    )
    part = dot(left, leg_own[...].reshape(own * rows, degrees), ((1,), (0,)))
    for i in range(n_lat):
        b_out[i] = part[:, LANES * i : LANES * (i + 1)]
    for other in lats:
        lat_copy(1, b_out.at[other], b_in.at[lat], other).start()
    b_in[lat] = b_out[lat]

    @pl.when(lat > 0)
    def _():
        high_rows.wait_recv()

    @pl.when(lat < n_lat - 1)
    def _():
        low_rows.wait_recv()

    deep = fields.shape[1]
    lane80 = lax.broadcasted_iota(jnp.int32, (deep, LANES), 1)
    packed_left = jnp.zeros((deep, LANES), jnp.float32)
    packed_right = jnp.zeros((deep, LANES), jnp.float32)
    for f in range(4):
        here = (lane80 >= 16 * f) & (lane80 < 16 * f + HALO)
        west = fields[f, :, 0:LANES]
        east = fields[f, :, base : base + LANES]
        packed_left = jnp.where(here, pltpu.roll(west, 16 * f, 1), packed_left)
        packed_right = jnp.where(
            here, pltpu.roll(east, (16 * f - (rest - HALO)) % LANES, 1), packed_right
        )
    to_left[...] = packed_left
    to_right[...] = packed_right
    west_side, east_side = lax.rem(lon + n_lon - 1, n_lon), lax.rem(lon + 1, n_lon)
    left_copy = edge_copy(4, to_left, from_right, (lat, west_side))
    right_copy = edge_copy(5, to_right, from_left, (lat, east_side))
    left_copy.start()
    right_copy.start()

    all_received(1, b_in, n_lat - 1)

    c_out[...] = jnp.sum(b_in[...], axis=0)
    for other in lats:
        lat_copy(2, c_out, c_in.at[lat], other).start()
    c_in[lat] = c_out[...]

    @pl.when(lat > 0)
    def _():
        low_rows.wait_send()

    @pl.when(lat < n_lat - 1)
    def _():
        high_rows.wait_send()

    left_copy.wait_recv()
    right_copy.wait_recv()
    right_halo = from_right[...]
    left_halo = from_left[...]
    for f in range(4):
        tile = fields[f, :, base : base + LANES]
        tile = jnp.where(
            (lane80 >= rest) & (lane80 < rest + HALO),
            pltpu.roll(right_halo, (rest - 16 * f) % LANES, 1),
            tile,
        )
        tile = jnp.where(
            lane80 >= LANES - HALO,
            pltpu.roll(left_halo, (LANES - HALO - 16 * f) % LANES, 1),
            tile,
        )
        fields[f, :, base : base + LANES] = tile

    @pl.when(lat > 0)
    def _():
        high_leg.wait_recv()

    @pl.when(lat < n_lat - 1)
    def _():
        low_leg.wait_recv()

    all_received(2, c_in, n_lat - 1)

    spectral = jnp.concatenate([c_in[i] for i in range(n_lat)], axis=1) * love_ref[...]
    inner = dot(spectral, leg_own[...].reshape(own * rows, degrees), ((1,), (1,)))
    outer = dot(spectral, leg_halo[...].reshape(own * 2 * HALO, degrees), ((1,), (1,)))
    body = jnp.zeros((8, LANES), jnp.float32)
    for h in range(own * rows // LANES):
        body = body + jnp.where(
            wave8 == 2 * h + lane8 // rows, inner[:, LANES * h : LANES * (h + 1)], 0.0
        )
    body = body + pltpu.roll(body, rows, 1)
    rim = jnp.concatenate(
        [outer, jnp.zeros((8, LANES - own * 2 * HALO), jnp.float32)], axis=1
    )
    rim = jnp.where(wave8 == lane8 // (2 * HALO), rim, 0.0)
    folded = pltpu.roll(rim, rows, 1)
    for m in range(1, own):
        folded = folded + pltpu.roll(rim, rows - 2 * HALO * m, 1)
    synthesized = jnp.where(
        lane8 < rows, body, jnp.where(lane8 < rows + 2 * HALO, folded, 0.0)
    )
    d_out[...] = synthesized * (1.0 / math.sqrt(count))
    for other in lons:
        lon_copy(3, d_out, d_in.at[lon], other).start()
    d_in[lon] = d_out[...]
    all_received(3, d_in, n_lon - 1)

    loading = dot(d_in[...].reshape(8 * n_lon, LANES), harmonics[...], ((0,), (0,)))[0:deep]

    surface = fields[0]
    east = fields[1]
    north = fields[2]
    wet = fields[3]
    wide, tall = width - 1, deep - 1
    for _ in range(SUBSTEPS):
        pressure = surface - loading
        east = wet * (
            east - EAST_STEP * (pltpu.roll(pressure, wide, 1) - pltpu.roll(pressure, 1, 1))
        )
        north = wet * (
            north - NORTH_STEP * (pltpu.roll(pressure, tall, 0) - pltpu.roll(pressure, 1, 0))
        )
        change = EAST_STEP * (pltpu.roll(east, wide, 1) - pltpu.roll(east, 1, 1)) + NORTH_STEP * (
            pltpu.roll(north, tall, 0) - pltpu.roll(north, 1, 0)
        )
        surface = surface - wet * change
    loading_out[...] = loading[0:rows, 0:cols]
    surface_out[...] = surface[0:rows, 0:cols]
    east_out_ref[...] = east[0:rows, 0:cols]
    north_out_ref[...] = north[0:rows, 0:cols]

    all_sent(0, a_in, n_lon - 1)
    all_sent(1, b_in, n_lat - 1)
    all_sent(2, c_in, n_lat - 1)
    all_sent(3, d_in, n_lon - 1)
    left_copy.wait_send()
    right_copy.wait_send()

    @pl.when(lat > 0)
    def _():
        low_leg.wait_send()

    @pl.when(lat < n_lat - 1)
    def _():
        high_leg.wait_send()


def write_kernel(a_ref, b_ref, c_ref, d_ref, a_out, b_out, c_out, d_out, sem):
    pairs = ((a_ref, a_out), (b_ref, b_out), (c_ref, c_out), (d_ref, d_out))
    copies = [pltpu.make_async_copy(src, dst, sem.at[k]) for k, (src, dst) in enumerate(pairs)]
    for copy in copies:
        copy.start()
    for copy in copies:
        copy.wait()


def shards(height, east_flow, north_flow, legendre, love_numbers, wavenumbers, land_sea):
    n_lat, n_lon = lax.axis_size("lat"), lax.axis_size("lon")
    rows, cols = height.shape
    own, _, degrees = legendre.shape
    width = -(-(cols + 2 * HALO) // LANES) * LANES
    deep = rows + 2 * HALO
    vmem = pl.BlockSpec(memory_space=pltpu.VMEM)
    f32 = jnp.float32
    shape = jax.ShapeDtypeStruct((rows, cols), f32)
    held = pltpu.VMEM((rows, cols), f32)
    results = pl.pallas_call(
        functools.partial(kernel, n_lat, n_lon),
        out_shape=(held, held, held, held),
        in_specs=[pl.BlockSpec(memory_space=pltpu.HBM)] * 7,
        out_specs=(vmem, vmem, vmem, vmem),
        scratch_shapes=[
            held,
            held,
            held,
            pltpu.VMEM((rows, cols), jnp.int32),
            pltpu.VMEM((1, degrees), f32),
            pltpu.VMEM((1, wavenumbers.shape[0]), jnp.int32),
            pltpu.VMEM((4, deep, width), f32),
            pltpu.VMEM((8 * n_lon, width), f32),
            pltpu.VMEM((2 * rows, width), f32),
            pltpu.VMEM((own, rows, degrees), f32),
            pltpu.VMEM((own, 2 * HALO, degrees), f32),
            pltpu.VMEM((n_lon, own, LANES), f32),
            pltpu.VMEM((n_lon, own, LANES), f32),
            pltpu.VMEM((n_lat, 8, LANES), f32),
            pltpu.VMEM((n_lat, 8, LANES), f32),
            pltpu.VMEM((8, LANES), f32),
            pltpu.VMEM((n_lat, 8, LANES), f32),
            pltpu.VMEM((8, LANES), f32),
            pltpu.VMEM((n_lon, 8, LANES), f32),
            pltpu.VMEM((deep, LANES), f32),
            pltpu.VMEM((deep, LANES), f32),
            pltpu.VMEM((deep, LANES), f32),
            pltpu.VMEM((deep, LANES), f32),
            pltpu.SemaphoreType.DMA((7,)),
            pltpu.SemaphoreType.DMA((4,)),
            pltpu.SemaphoreType.DMA((4,)),
            pltpu.SemaphoreType.DMA((6,)),
            pltpu.SemaphoreType.DMA((6,)),
        ],
        compiler_params=pltpu.CompilerParams(
            collective_id=0, has_side_effects=True, vmem_limit_bytes=24 << 20
        ),
    )(
        *[
            pltpu.with_memory_space_constraint(x, pltpu.HBM)
            for x in (
                height,
                east_flow,
                north_flow,
                land_sea,
                legendre,
                love_numbers.reshape(1, degrees),
                wavenumbers.reshape(1, wavenumbers.shape[0]),
            )
        ]
    )
    anywhere = pl.BlockSpec(memory_space=pl.ANY)
    return pl.pallas_call(
        write_kernel,
        out_shape=(shape, shape, shape, shape),
        in_specs=[vmem, vmem, vmem, vmem],
        out_specs=(anywhere, anywhere, anywhere, anywhere),
        scratch_shapes=[pltpu.SemaphoreType.DMA((4,))],
        compiler_params=pltpu.CompilerParams(vmem_limit_bytes=8 << 20),
    )(*results)


def solution(mesh):
    return jax.shard_map(
        shards,
        mesh=mesh,
        in_specs=(
            P("lat", "lon"),
            P("lat", "lon"),
            P("lat", "lon"),
            P("lon", "lat", None),
            P(),
            P(),
            P("lat", "lon"),
        ),
        out_specs=(P("lat", "lon"), P("lat", "lon"), P("lat", "lon"), P("lat", "lon")),
        check_vma=False,
    )
```

```python
import functools
import math

import jax
import jax.numpy as jnp
from jax import lax
from jax.experimental import pallas as pl
from jax.experimental.pallas import tpu as pltpu
from jax.sharding import PartitionSpec as P

SUBSTEPS = 4
HALO = 2 * SUBSTEPS
LANES = 128
STEP = 0.3
MESH = pl.DeviceIdType.MESH


def dot(a, b, dims):
    return lax.dot_general(a, b, (dims, ((), ())), preferred_element_type=jnp.float32)


def split(x):
    high = x.astype(jnp.bfloat16)
    return high, (x - high.astype(jnp.float32)).astype(jnp.bfloat16)


def stacked(x):
    return jnp.concatenate([x, x - x.astype(jnp.bfloat16).astype(jnp.float32)], axis=0).astype(
        jnp.bfloat16
    )


def ring_order(n):
    return sorted(range(n), key=lambda d: -min(d, n - d))


def lat_partners(n_lat, lat):
    n_y = min(8, n_lat)
    x_hi, y = lat // n_y, lat % n_y
    steps = [(dx, dy) for dx in range(n_lat // n_y) for dy in range(n_y) if dx or dy]
    steps.sort(key=lambda s: -(2 * s[0] + min(s[1], n_y - s[1])))
    n_x = n_lat // n_y
    return [((x_hi + dx) % n_x) * n_y + (y + dy) % n_y for dx, dy in steps]


def lon_partners(n_lon, lon):
    n_z = n_lon // 4
    z, low = lon // 4, lon % 4
    steps = [(dz, e) for dz in ring_order(n_z) for e in (2, 3, 1, 0) if dz or e]
    return [((z + dz) % n_z) * 4 + (low + e) % 4 for dz, e in steps]


def kernel(
    n_lat,
    n_lon,
    height_hbm,
    east_hbm,
    north_hbm,
    land_hbm,
    legendre_ref,
    love_hbm,
    waves_hbm,
    loading_out,
    surface_out,
    east_out_ref,
    north_out_ref,
    height_ref,
    east_ref,
    north_ref,
    land_ref,
    love_ref,
    waves_ref,
    fields,
    by_slot,
    harm_high,
    harm_low,
    leg_own,
    leg_high,
    leg_low,
    leg_halo,
    a_out,
    a_in,
    b_out,
    b_in,
    c_out,
    c_in,
    d_out,
    d_in,
    to_left,
    to_right,
    from_right,
    from_left,
    in_sem,
    send_sem,
    recv_sem,
    edge_send,
    edge_recv,
):
    lat = lax.axis_index("lat")
    lon = lax.axis_index("lon")
    rows, cols = height_ref.shape
    own = legendre_ref.shape[0]
    width = fields.shape[2]
    period = cols * n_lon
    base, rest = cols // LANES * LANES, cols % LANES
    lats = lat_partners(n_lat, lat)
    lons = lon_partners(n_lon, lon)

    inputs = [
        pltpu.make_async_copy(src, dst, in_sem.at[k])
        for k, (src, dst) in enumerate(
            (
                (waves_hbm, waves_ref),
                (height_hbm, height_ref),
                (east_hbm, east_ref),
                (north_hbm, north_ref),
                (land_hbm, land_ref),
                (love_hbm, love_ref),
                (legendre_ref, leg_own),
            )
        )
    ]
    for copy in inputs:
        copy.start()
    barrier = pltpu.get_barrier_semaphore()
    for other in lons:
        pl.semaphore_signal(barrier, inc=1, device_id=(lat, other), device_id_type=MESH)
    for other in lats:
        pl.semaphore_signal(barrier, inc=1, device_id=(other, lon), device_id_type=MESH)
    for copy in inputs[:6]:
        copy.wait()

    for f, ref in enumerate((height_ref, east_ref, north_ref, land_ref)):
        fields[f, 0:rows, base:width] = jnp.zeros((rows, width - base), jnp.float32)
        fields[f, 0:rows, 0:cols] = ref[...].astype(jnp.float32)
    high, low = split(fields[0, 0:rows, :])
    twice_high = jnp.concatenate([high, high], axis=0)
    twice_low = jnp.concatenate([low, low], axis=0)

    count = waves_ref.shape[1]
    by_slot[...] = jnp.broadcast_to(waves_ref[...].astype(jnp.float32), (LANES, count)).T
    waves = jnp.concatenate([by_slot[pl.ds(m, n_lon, stride=own), :] for m in range(own)], axis=0)
    start = jnp.bitwise_and(waves.astype(jnp.int32) * lon, n_lon - 1).astype(jnp.float32) * cols
    quarter = period // 4
    lane = lax.broadcasted_iota(jnp.int32, (16, width), 1)
    column = jnp.where(lane < width - 64, lane, lane - width).astype(jnp.float32)
    for g in range(count // 16):
        here = slice(16 * g, 16 * g + 16)
        wave = jnp.concatenate([waves[here]] * (width // LANES), axis=1)
        first = jnp.concatenate([start[here]] * (width // LANES), axis=1)
        r = wave * column + first
        turn = (r * (1.0 / quarter) + 4096.5).astype(jnp.int32)
        d = r - (turn - 4096).astype(jnp.float32) * quarter
        phi = d * (2.0 * math.pi / period)
        s = phi * phi
        sin = 1.0 / 362880.0
        sin = sin * s - 1.0 / 5040.0
        sin = sin * s + 1.0 / 120.0
        sin = sin * s - 1.0 / 6.0
        sin = phi + phi * (s * sin)
        cos = -1.0 / 3628800.0
        cos = cos * s + 1.0 / 40320.0
        cos = cos * s - 1.0 / 720.0
        cos = cos * s + 1.0 / 24.0
        cos = cos * s - 0.5
        cos = 1.0 + s * cos
        odd = jnp.bitwise_and(turn, 1) == 1
        cos_minus = jnp.bitwise_and(turn + 1, 2) == 2
        sin_minus = jnp.bitwise_and(turn, 2) == 2
        c = jnp.where(odd, sin, cos)
        c = jnp.where(cos_minus, -c, c)
        n = jnp.where(odd, cos, sin)
        n = jnp.where(sin_minus, -n, n)
        there = slice(count + 16 * g, count + 16 * g + 16)
        harm_high[here, :], harm_low[here, :] = split(c)
        harm_high[there, :], harm_low[there, :] = split(n)

    partial = (
        dot(harm_high[...], twice_high, ((1,), (1,)))
        + dot(harm_high[...], twice_low, ((1,), (1,)))
        + dot(harm_low[...], twice_high, ((1,), (1,)))
    )
    half = lax.broadcasted_iota(jnp.int32, (count, LANES), 1) < rows
    partial = jnp.where(half, partial[0:count], partial[count : 2 * count])
    for m in range(own):
        a_out[:, m, :] = partial[n_lon * m : n_lon * (m + 1)]

    pl.semaphore_wait(barrier, n_lat + n_lon - 2)

    def lon_copy(k, src, dst, other):
        return pltpu.make_async_remote_copy(
            src_ref=src,
            dst_ref=dst,
            send_sem=send_sem.at[k],
            recv_sem=recv_sem.at[k],
            device_id=(lat, other),
            device_id_type=MESH,
        )

    def lat_copy(k, src, dst, other):
        return pltpu.make_async_remote_copy(
            src_ref=src,
            dst_ref=dst,
            send_sem=send_sem.at[k],
            recv_sem=recv_sem.at[k],
            device_id=(other, lon),
            device_id_type=MESH,
        )

    def all_received(k, ref, n):
        pltpu.make_async_copy(ref.at[pl.ds(0, n)], ref.at[pl.ds(0, n)], recv_sem.at[k]).wait()

    def all_sent(k, ref, n):
        pltpu.make_async_copy(ref.at[pl.ds(0, n)], ref.at[pl.ds(0, n)], send_sem.at[k]).wait()

    for other in lons:
        lon_copy(0, a_out.at[other], a_in.at[lon], other).start()
    a_in[lon] = a_out[lon]

    below, above = jnp.minimum(lat + 1, n_lat - 1), jnp.maximum(lat - 1, 0)

    def edge_copy(k, src, dst, where):
        return pltpu.make_async_remote_copy(
            src_ref=src,
            dst_ref=dst,
            send_sem=edge_send.at[k],
            recv_sem=edge_recv.at[k],
            device_id=where,
            device_id_type=MESH,
        )

    low_rows = edge_copy(
        0, fields.at[:, 0:HALO, :], fields.at[:, rows : rows + HALO, :], (above, lon)
    )
    high_rows = edge_copy(
        1,
        fields.at[:, rows - HALO : rows, :],
        fields.at[:, rows + HALO : rows + 2 * HALO, :],
        (below, lon),
    )
    low_leg = edge_copy(
        2, legendre_ref.at[:, 0:HALO, :], leg_halo.at[:, 0:HALO, :], (above, lon)
    )
    high_leg = edge_copy(
        3,
        legendre_ref.at[:, rows - HALO : rows, :],
        leg_halo.at[:, HALO : 2 * HALO, :],
        (below, lon),
    )

    @pl.when(lat > 0)
    def _():
        low_rows.start()
        low_leg.start()

    @pl.when(lat < n_lat - 1)
    def _():
        high_rows.start()
        high_leg.start()

    @pl.when(lat == 0)
    def _():
        fields[:, rows + HALO : rows + 2 * HALO, :] = jnp.zeros((4, HALO, width), jnp.float32)
        leg_halo[:, HALO : 2 * HALO, :] = jnp.zeros((own, HALO, leg_halo.shape[2]), jnp.float32)

    @pl.when(lat == n_lat - 1)
    def _():
        fields[:, rows : rows + HALO, :] = jnp.zeros((4, HALO, width), jnp.float32)
        leg_halo[:, 0:HALO, :] = jnp.zeros((own, HALO, leg_halo.shape[2]), jnp.float32)

    inputs[6].wait()
    inner_rows = own * rows
    for m in range(own):
        here = slice(rows * m, rows * (m + 1))
        leg_high[here, :], leg_low[here, :] = split(leg_own[m])
    all_received(0, a_in, n_lon - 1)
    fourier = jnp.sum(a_in[...], axis=0) * (1.0 / math.sqrt(period))

    degrees = leg_own.shape[2]
    lane8 = lax.broadcasted_iota(jnp.int32, (8, LANES), 1)
    row8 = lax.broadcasted_iota(jnp.int32, (8, LANES), 0)
    both = jnp.concatenate([fourier, fourier], axis=0)
    swapped = pltpu.roll(both, rows, 1)
    spread = jnp.where((lane8 < rows) == (row8 < 4), both, swapped)
    wave8 = jnp.bitwise_and(row8, 3)
    left = jnp.concatenate(
        [jnp.where(wave8 == 2 * h + lane8 // rows, spread, 0.0) for h in range(own * rows // LANES)],
        axis=1,
    )
    left = stacked(left)
    part = dot(left, leg_high[0:inner_rows, :], ((1,), (0,)))
    part = part[0:8] + part[8:16] + dot(left[0:8], leg_low[0:inner_rows, :], ((1,), (0,)))
    for i in range(n_lat):
        b_out[i] = part[:, LANES * i : LANES * (i + 1)]
    for other in lats:
        lat_copy(1, b_out.at[other], b_in.at[lat], other).start()
    b_in[lat] = b_out[lat]

    @pl.when(lat > 0)
    def _():
        high_rows.wait_recv()

    @pl.when(lat < n_lat - 1)
    def _():
        low_rows.wait_recv()

    deep = fields.shape[1]
    lane80 = lax.broadcasted_iota(jnp.int32, (deep, LANES), 1)
    packed_left = jnp.zeros((deep, LANES), jnp.float32)
    packed_right = jnp.zeros((deep, LANES), jnp.float32)
    for f in range(4):
        here = (lane80 >= 16 * f) & (lane80 < 16 * f + HALO)
        west = fields[f, :, 0:LANES]
        east = fields[f, :, base : base + LANES]
        packed_left = jnp.where(here, pltpu.roll(west, 16 * f, 1), packed_left)
        packed_right = jnp.where(
            here, pltpu.roll(east, (16 * f - (rest - HALO)) % LANES, 1), packed_right
        )
    to_left[...] = packed_left
    to_right[...] = packed_right
    west_side, east_side = lax.rem(lon + n_lon - 1, n_lon), lax.rem(lon + 1, n_lon)
    left_copy = edge_copy(4, to_left, from_right, (lat, west_side))
    right_copy = edge_copy(5, to_right, from_left, (lat, east_side))
    left_copy.start()
    right_copy.start()

    all_received(1, b_in, n_lat - 1)

    c_out[...] = jnp.sum(b_in[...], axis=0)
    for other in lats:
        lat_copy(2, c_out, c_in.at[lat], other).start()
    c_in[lat] = c_out[...]

    @pl.when(lat > 0)
    def _():
        low_rows.wait_send()

    @pl.when(lat < n_lat - 1)
    def _():
        high_rows.wait_send()

    left_copy.wait_recv()
    right_copy.wait_recv()
    right_halo = from_right[...]
    left_halo = from_left[...]
    for f in range(4):
        tile = fields[f, :, base : base + LANES]
        tile = jnp.where(
            (lane80 >= rest) & (lane80 < rest + HALO),
            pltpu.roll(right_halo, (rest - 16 * f) % LANES, 1),
            tile,
        )
        tile = jnp.where(
            lane80 >= LANES - HALO,
            pltpu.roll(left_halo, (LANES - HALO - 16 * f) % LANES, 1),
            tile,
        )
        fields[f, :, base : base + LANES] = tile

    @pl.when(lat > 0)
    def _():
        high_leg.wait_recv()

    @pl.when(lat < n_lat - 1)
    def _():
        low_leg.wait_recv()

    both_leg = split(leg_halo[...].reshape(own * 2 * HALO, degrees))
    leg_high[inner_rows:, :], leg_low[inner_rows:, :] = both_leg
    all_received(2, c_in, n_lat - 1)

    spectral = jnp.concatenate([c_in[i] for i in range(n_lat)], axis=1) * love_ref[...]
    spectral = stacked(spectral)
    values = dot(spectral, leg_high[...], ((1,), (1,)))
    values = values[0:8] + values[8:16] + dot(spectral[0:8], leg_low[...], ((1,), (1,)))
    body = jnp.zeros((8, LANES), jnp.float32)
    for h in range(inner_rows // LANES):
        body = body + jnp.where(
            wave8 == 2 * h + lane8 // rows, values[:, LANES * h : LANES * (h + 1)], 0.0
        )
    body = body + pltpu.roll(body, rows, 1)
    body = jnp.where(lane8 < rows, body, pltpu.roll(body, 4, 0))
    rim = jnp.concatenate(
        [values[:, inner_rows:], jnp.zeros((8, LANES - own * 2 * HALO), jnp.float32)], axis=1
    )
    rim = jnp.where(wave8 == lane8 // (2 * HALO), rim, 0.0)
    rim = jnp.where(row8 < 4, rim, pltpu.roll(rim, own * 2 * HALO, 1))
    rim = jnp.sum(rim, axis=0, keepdims=True)
    packet = jnp.where(row8 < 4, body, rim) * (1.0 / math.sqrt(count))
    d_out[...] = packet[0:5]
    for other in lons:
        lon_copy(3, d_out, d_in.at[lon], other).start()
    d_in[lon] = d_out[...]

    wet = fields[3]
    fields[1] = fields[1] * wet
    fields[2] = fields[2] * wet
    fields[3] = wet * STEP
    all_received(3, d_in, n_lon - 1)

    rows_kt = jnp.concatenate([d_in[:, m, :] for m in range(own)], axis=0)
    rows_tk = rows_kt.T
    rim_kt = jnp.concatenate(
        [d_in[:, 4, :], jnp.zeros((count - n_lon, LANES), jnp.float32)], axis=0
    )
    rim_tk = rim_kt.T
    rims = []
    for p in range(2):
        side = rim_tk[2 * HALO * own * p : 2 * HALO * (own * p + 1)]
        for m in range(1, own):
            first = 2 * HALO * (own * p + m)
            side = side + pltpu.roll(rim_tk[first : first + 2 * HALO], n_lon * m, 1)
        rims.append(side)
    coefficients = jnp.concatenate(
        [
            jnp.concatenate([rows_tk[0:rows], rows_tk[rows : 2 * rows]], axis=1),
            jnp.concatenate(rims, axis=1),
        ],
        axis=0,
    )
    coefficients = stacked(coefficients)
    loading = dot(coefficients, harm_high[...], ((1,), (0,)))
    loading = (
        loading[0:deep]
        + loading[deep : 2 * deep]
        + dot(coefficients[0:deep], harm_low[...], ((1,), (0,)))
    )

    pressure = fields[0] - loading
    east = fields[1]
    north = fields[2]
    step = fields[3]
    wide, tall = width - 1, deep - 1
    for _ in range(SUBSTEPS):
        east = east - step * (pltpu.roll(pressure, wide, 1) - pltpu.roll(pressure, 1, 1))
        north = north - step * (pltpu.roll(pressure, tall, 0) - pltpu.roll(pressure, 1, 0))
        pressure = pressure - step * (
            (pltpu.roll(east, wide, 1) - pltpu.roll(east, 1, 1))
            + (pltpu.roll(north, tall, 0) - pltpu.roll(north, 1, 0))
        )
    surface = pressure + loading
    loading_out[...] = loading[0:rows, 0:cols]
    surface_out[...] = surface[0:rows, 0:cols]
    east_out_ref[...] = east[0:rows, 0:cols]
    north_out_ref[...] = north[0:rows, 0:cols]

    all_sent(0, a_in, n_lon - 1)
    all_sent(1, b_in, n_lat - 1)
    all_sent(2, c_in, n_lat - 1)
    all_sent(3, d_in, n_lon - 1)
    left_copy.wait_send()
    right_copy.wait_send()

    @pl.when(lat > 0)
    def _():
        low_leg.wait_send()

    @pl.when(lat < n_lat - 1)
    def _():
        high_leg.wait_send()


def write_kernel(a_ref, b_ref, c_ref, d_ref, a_out, b_out, c_out, d_out, sem):
    pairs = ((a_ref, a_out), (b_ref, b_out), (c_ref, c_out), (d_ref, d_out))
    copies = [pltpu.make_async_copy(src, dst, sem.at[k]) for k, (src, dst) in enumerate(pairs)]
    for copy in copies:
        copy.start()
    for copy in copies:
        copy.wait()


def shards(height, east_flow, north_flow, legendre, love_numbers, wavenumbers, land_sea):
    n_lat, n_lon = lax.axis_size("lat"), lax.axis_size("lon")
    rows, cols = height.shape
    own, _, degrees = legendre.shape
    width = -(-(cols + 2 * HALO) // LANES) * LANES
    deep = rows + 2 * HALO
    vmem = pl.BlockSpec(memory_space=pltpu.VMEM)
    f32 = jnp.float32
    shape = jax.ShapeDtypeStruct((rows, cols), f32)
    held = pltpu.VMEM((rows, cols), f32)
    results = pl.pallas_call(
        functools.partial(kernel, n_lat, n_lon),
        out_shape=(held, held, held, held),
        in_specs=[pl.BlockSpec(memory_space=pltpu.HBM)] * 7,
        out_specs=(vmem, vmem, vmem, vmem),
        scratch_shapes=[
            held,
            held,
            held,
            pltpu.VMEM((rows, cols), jnp.int32),
            pltpu.VMEM((1, degrees), f32),
            pltpu.VMEM((1, wavenumbers.shape[0]), jnp.int32),
            pltpu.VMEM((4, deep, width), f32),
            pltpu.VMEM((own * n_lon, LANES), f32),
            pltpu.VMEM((2 * own * n_lon, width), jnp.bfloat16),
            pltpu.VMEM((2 * own * n_lon, width), jnp.bfloat16),
            pltpu.VMEM((own, rows, degrees), f32),
            pltpu.VMEM((own * deep, degrees), jnp.bfloat16),
            pltpu.VMEM((own * deep, degrees), jnp.bfloat16),
            pltpu.VMEM((own, 2 * HALO, degrees), f32),
            pltpu.VMEM((n_lon, own, LANES), f32),
            pltpu.VMEM((n_lon, own, LANES), f32),
            pltpu.VMEM((n_lat, 8, LANES), f32),
            pltpu.VMEM((n_lat, 8, LANES), f32),
            pltpu.VMEM((8, LANES), f32),
            pltpu.VMEM((n_lat, 8, LANES), f32),
            pltpu.VMEM((5, LANES), f32),
            pltpu.VMEM((n_lon, 5, LANES), f32),
            pltpu.VMEM((deep, LANES), f32),
            pltpu.VMEM((deep, LANES), f32),
            pltpu.VMEM((deep, LANES), f32),
            pltpu.VMEM((deep, LANES), f32),
            pltpu.SemaphoreType.DMA((7,)),
            pltpu.SemaphoreType.DMA((4,)),
            pltpu.SemaphoreType.DMA((4,)),
            pltpu.SemaphoreType.DMA((6,)),
            pltpu.SemaphoreType.DMA((6,)),
        ],
        compiler_params=pltpu.CompilerParams(
            collective_id=0, has_side_effects=True, vmem_limit_bytes=24 << 20
        ),
    )(
        *[
            pltpu.with_memory_space_constraint(x, pltpu.HBM)
            for x in (
                height,
                east_flow,
                north_flow,
                land_sea,
                legendre,
                love_numbers.reshape(1, degrees),
                wavenumbers.reshape(1, wavenumbers.shape[0]),
            )
        ]
    )
    anywhere = pl.BlockSpec(memory_space=pl.ANY)
    return pl.pallas_call(
        write_kernel,
        out_shape=(shape, shape, shape, shape),
        in_specs=[vmem, vmem, vmem, vmem],
        out_specs=(anywhere, anywhere, anywhere, anywhere),
        scratch_shapes=[pltpu.SemaphoreType.DMA((4,))],
        compiler_params=pltpu.CompilerParams(vmem_limit_bytes=8 << 20),
    )(*results)


def solution(mesh):
    return jax.shard_map(
        shards,
        mesh=mesh,
        in_specs=(
            P("lat", "lon"),
            P("lat", "lon"),
            P("lat", "lon"),
            P("lon", "lat", None),
            P(),
            P(),
            P("lat", "lon"),
        ),
        out_specs=(P("lat", "lon"), P("lat", "lon"), P("lat", "lon"), P("lat", "lon")),
        check_vma=False,
    )
```

```python
import functools
import math

import jax
import jax.numpy as jnp
from jax import lax
from jax.experimental import pallas as pl
from jax.experimental.pallas import tpu as pltpu
from jax.sharding import PartitionSpec as P

SUBSTEPS = 4
HALO = 2 * SUBSTEPS
LANES = 128
STEP = 0.3
MESH = pl.DeviceIdType.MESH


def dot(a, b, dims):
    return lax.dot_general(a, b, (dims, ((), ())), preferred_element_type=jnp.float32)


def split(x):
    high = x.astype(jnp.bfloat16)
    return high, (x - high.astype(jnp.float32)).astype(jnp.bfloat16)


def stacked(x):
    return jnp.concatenate([x, x - x.astype(jnp.bfloat16).astype(jnp.float32)], axis=0).astype(
        jnp.bfloat16
    )


def hops(n, d):
    return min(d, n - d)


def lat_partners(n_lat, lat):
    n_y = n_lat // 2
    x_hi, y = lax.div(lat, n_y), lax.rem(lat, n_y)
    steps = [(2 * dx + hops(n_y, dy), dx, dy) for dx in range(2) for dy in range(n_y)]
    steps = sorted((step for step in steps if step[0]), reverse=True)
    return [
        (far, (1 - x_hi if dx else x_hi) * n_y + lax.rem(y + dy, n_y)) for far, dx, dy in steps
    ]


def lon_partners(n_lon, lon):
    n_z = n_lon // 4
    z, x_lo, core = lax.div(lon, 4), lax.rem(lax.div(lon, 2), 2), lax.rem(lon, 2)
    steps = [
        (hops(n_z, dz) + dx, dz, dx, dc)
        for dz in range(n_z)
        for dx in range(2)
        for dc in range(2)
        if dz or dx or dc
    ]
    return [
        (
            far,
            lax.rem(z + dz, n_z) * 4 + (1 - x_lo if dx else x_lo) * 2 + (1 - core if dc else core),
        )
        for far, dz, dx, dc in sorted(steps, reverse=True)
    ]


def kernel(
    n_lat,
    n_lon,
    height_hbm,
    east_hbm,
    north_hbm,
    land_hbm,
    legendre_ref,
    love_hbm,
    waves_hbm,
    loading_out,
    surface_out,
    east_out_ref,
    north_out_ref,
    height_ref,
    east_ref,
    north_ref,
    land_ref,
    love_ref,
    waves_ref,
    fields,
    by_slot,
    harm_high,
    harm_low,
    leg_own,
    leg_high,
    leg_low,
    leg_halo,
    a_out,
    a_in,
    b_out,
    b_in,
    c_out,
    c_in,
    d_out,
    d_in,
    to_left,
    to_right,
    from_right,
    from_left,
    in_sem,
    send_sem,
    recv_sem,
    edge_send,
    edge_recv,
    c_send,
    c_recv,
):
    lat = lax.axis_index("lat")
    lon = lax.axis_index("lon")
    rows, cols = height_ref.shape
    own = legendre_ref.shape[0]
    width = fields.shape[2]
    period = cols * n_lon
    base, rest = cols // LANES * LANES, cols % LANES
    lats = lat_partners(n_lat, lat)
    lons = lon_partners(n_lon, lon)

    inputs = [
        pltpu.make_async_copy(src, dst, in_sem.at[k])
        for k, (src, dst) in enumerate(
            (
                (waves_hbm, waves_ref),
                (height_hbm, height_ref),
                (east_hbm, east_ref),
                (north_hbm, north_ref),
                (land_hbm, land_ref),
                (love_hbm, love_ref),
                (legendre_ref, leg_own),
            )
        )
    ]
    for copy in inputs:
        copy.start()
    barrier = pltpu.get_barrier_semaphore()
    everyone = [(far, (other, lon)) for far, other in lats]
    everyone += [(far, (lat, other)) for far, other in lons]
    for _, where in sorted(everyone, key=lambda other: -other[0]):
        pl.semaphore_signal(barrier, inc=1, device_id=where, device_id_type=MESH)
    n_y = n_lat // 2
    y = lax.rem(lat, n_y)
    for copy in inputs[:6]:
        copy.wait()

    for f, ref in enumerate((height_ref, east_ref, north_ref, land_ref)):
        fields[f, 0:rows, base:width] = jnp.zeros((rows, width - base), jnp.float32)
        fields[f, 0:rows, 0:cols] = ref[...].astype(jnp.float32)
    high, low = split(fields[0, 0:rows, :])
    twice_high = jnp.concatenate([high, high], axis=0)
    twice_low = jnp.concatenate([low, low], axis=0)

    count = waves_ref.shape[1]
    by_slot[...] = jnp.broadcast_to(waves_ref[...].astype(jnp.float32), (LANES, count)).T
    waves = jnp.concatenate([by_slot[pl.ds(m, n_lon, stride=own), :] for m in range(own)], axis=0)
    start = jnp.bitwise_and(waves.astype(jnp.int32) * lon, n_lon - 1).astype(jnp.float32) * cols
    quarter = period // 4
    lane = lax.broadcasted_iota(jnp.int32, (16, width), 1)
    column = jnp.where(lane < width - 64, lane, lane - width).astype(jnp.float32)
    for g in range(count // 16):
        here = slice(16 * g, 16 * g + 16)
        wave = jnp.concatenate([waves[here]] * (width // LANES), axis=1)
        first = jnp.concatenate([start[here]] * (width // LANES), axis=1)
        r = wave * column + first
        turn = (r * (1.0 / quarter) + 4096.5).astype(jnp.int32)
        d = r - (turn - 4096).astype(jnp.float32) * quarter
        phi = d * (2.0 * math.pi / period)
        s = phi * phi
        sin = 1.0 / 362880.0
        sin = sin * s - 1.0 / 5040.0
        sin = sin * s + 1.0 / 120.0
        sin = sin * s - 1.0 / 6.0
        sin = phi + phi * (s * sin)
        cos = -1.0 / 3628800.0
        cos = cos * s + 1.0 / 40320.0
        cos = cos * s - 1.0 / 720.0
        cos = cos * s + 1.0 / 24.0
        cos = cos * s - 0.5
        cos = 1.0 + s * cos
        odd = jnp.bitwise_and(turn, 1) == 1
        cos_minus = jnp.bitwise_and(turn + 1, 2) == 2
        sin_minus = jnp.bitwise_and(turn, 2) == 2
        c = jnp.where(odd, sin, cos)
        c = jnp.where(cos_minus, -c, c)
        n = jnp.where(odd, cos, sin)
        n = jnp.where(sin_minus, -n, n)
        there = slice(count + 16 * g, count + 16 * g + 16)
        harm_high[here, :], harm_low[here, :] = split(c)
        harm_high[there, :], harm_low[there, :] = split(n)

    partial = (
        dot(harm_high[...], twice_high, ((1,), (1,)))
        + dot(harm_high[...], twice_low, ((1,), (1,)))
        + dot(harm_low[...], twice_high, ((1,), (1,)))
    )
    half = lax.broadcasted_iota(jnp.int32, (count, LANES), 1) < rows
    partial = jnp.where(half, partial[0:count], partial[count : 2 * count])
    for m in range(own):
        a_out[:, m, :] = partial[n_lon * m : n_lon * (m + 1)]

    pl.semaphore_wait(barrier, n_lat + n_lon - 2)

    def lon_copy(k, src, dst, other):
        return pltpu.make_async_remote_copy(
            src_ref=src,
            dst_ref=dst,
            send_sem=send_sem.at[k],
            recv_sem=recv_sem.at[k],
            device_id=(lat, other),
            device_id_type=MESH,
        )

    def lat_copy(k, src, dst, other):
        return pltpu.make_async_remote_copy(
            src_ref=src,
            dst_ref=dst,
            send_sem=send_sem.at[k],
            recv_sem=recv_sem.at[k],
            device_id=(other, lon),
            device_id_type=MESH,
        )

    def all_received(k, ref, n):
        pltpu.make_async_copy(ref.at[pl.ds(0, n)], ref.at[pl.ds(0, n)], recv_sem.at[k]).wait()

    def all_sent(k, ref, n):
        pltpu.make_async_copy(ref.at[pl.ds(0, n)], ref.at[pl.ds(0, n)], send_sem.at[k]).wait()

    for _, other in lons:
        lon_copy(0, a_out.at[other], a_in.at[lon], other).start()
    a_in[lon] = a_out[lon]

    below, above = jnp.minimum(lat + 1, n_lat - 1), jnp.maximum(lat - 1, 0)

    def edge_copy(k, src, dst, where):
        return pltpu.make_async_remote_copy(
            src_ref=src,
            dst_ref=dst,
            send_sem=edge_send.at[k],
            recv_sem=edge_recv.at[k],
            device_id=where,
            device_id_type=MESH,
        )

    low_rows = edge_copy(
        0, fields.at[:, 0:HALO, :], fields.at[:, rows : rows + HALO, :], (above, lon)
    )
    high_rows = edge_copy(
        1,
        fields.at[:, rows - HALO : rows, :],
        fields.at[:, rows + HALO : rows + 2 * HALO, :],
        (below, lon),
    )
    low_leg = edge_copy(
        2, legendre_ref.at[:, 0:HALO, :], leg_halo.at[:, 0:HALO, :], (above, lon)
    )
    high_leg = edge_copy(
        3,
        legendre_ref.at[:, rows - HALO : rows, :],
        leg_halo.at[:, HALO : 2 * HALO, :],
        (below, lon),
    )

    @pl.when(lat > 0)
    def _():
        low_rows.start()
        low_leg.start()

    @pl.when(lat < n_lat - 1)
    def _():
        high_rows.start()
        high_leg.start()

    @pl.when(lat == 0)
    def _():
        fields[:, rows + HALO : rows + 2 * HALO, :] = jnp.zeros((4, HALO, width), jnp.float32)
        leg_halo[:, HALO : 2 * HALO, :] = jnp.zeros((own, HALO, leg_halo.shape[2]), jnp.float32)

    @pl.when(lat == n_lat - 1)
    def _():
        fields[:, rows : rows + HALO, :] = jnp.zeros((4, HALO, width), jnp.float32)
        leg_halo[:, 0:HALO, :] = jnp.zeros((own, HALO, leg_halo.shape[2]), jnp.float32)

    inputs[6].wait()
    inner_rows = own * rows
    for m in range(own):
        here = slice(rows * m, rows * (m + 1))
        leg_high[here, :], leg_low[here, :] = split(leg_own[m])
    all_received(0, a_in, n_lon - 1)
    fourier = jnp.sum(a_in[...], axis=0) * (1.0 / math.sqrt(period))

    degrees = leg_own.shape[2]
    lane8 = lax.broadcasted_iota(jnp.int32, (8, LANES), 1)
    row8 = lax.broadcasted_iota(jnp.int32, (8, LANES), 0)
    both = jnp.concatenate([fourier, fourier], axis=0)
    swapped = pltpu.roll(both, rows, 1)
    spread = jnp.where((lane8 < rows) == (row8 < 4), both, swapped)
    wave8 = jnp.bitwise_and(row8, 3)
    left = jnp.concatenate(
        [jnp.where(wave8 == 2 * h + lane8 // rows, spread, 0.0) for h in range(own * rows // LANES)],
        axis=1,
    )
    left = stacked(left)
    part = dot(left, leg_high[0:inner_rows, :], ((1,), (0,)))
    part = part[0:8] + part[8:16] + dot(left[0:8], leg_low[0:inner_rows, :], ((1,), (0,)))
    chunk = degrees // n_y
    for i in range(n_y):
        b_out[i] = part[:, chunk * i : chunk * (i + 1)]
    for _, other in lats:
        lat_copy(1, b_out.at[lax.rem(other, n_y)], b_in.at[lat], other).start()
    b_in[lat] = b_out[y]

    @pl.when(lat > 0)
    def _():
        high_rows.wait_recv()

    @pl.when(lat < n_lat - 1)
    def _():
        low_rows.wait_recv()

    deep = fields.shape[1]
    lane80 = lax.broadcasted_iota(jnp.int32, (deep, LANES), 1)
    packed_left = jnp.zeros((deep, LANES), jnp.float32)
    packed_right = jnp.zeros((deep, LANES), jnp.float32)
    for f in range(4):
        here = (lane80 >= 16 * f) & (lane80 < 16 * f + HALO)
        west = fields[f, :, 0:LANES]
        east = fields[f, :, base : base + LANES]
        packed_left = jnp.where(here, pltpu.roll(west, 16 * f, 1), packed_left)
        packed_right = jnp.where(
            here, pltpu.roll(east, (16 * f - (rest - HALO)) % LANES, 1), packed_right
        )
    to_left[...] = packed_left
    to_right[...] = packed_right
    west_side, east_side = lax.rem(lon + n_lon - 1, n_lon), lax.rem(lon + 1, n_lon)
    left_copy = edge_copy(4, to_left, from_right, (lat, west_side))
    right_copy = edge_copy(5, to_right, from_left, (lat, east_side))
    left_copy.start()
    right_copy.start()

    all_received(1, b_in, n_lat - 1)

    c_out[...] = jnp.sum(b_in[...], axis=0)
    bands = sorted(range(1, n_y), key=lambda dy: -hops(n_y, dy))
    c_copies = [
        pltpu.make_async_remote_copy(
            src_ref=c_out,
            dst_ref=c_in.at[y],
            send_sem=c_send.at[dy],
            recv_sem=c_recv.at[n_y - dy],
            device_id=(lat - y + lax.rem(y + dy, n_y), lon),
            device_id_type=MESH,
        )
        for dy in bands
    ]
    for copy in c_copies:
        copy.start()

    @pl.when(lat > 0)
    def _():
        low_rows.wait_send()

    @pl.when(lat < n_lat - 1)
    def _():
        high_rows.wait_send()

    left_copy.wait_recv()
    right_copy.wait_recv()
    right_halo = from_right[...]
    left_halo = from_left[...]
    for f in range(4):
        tile = fields[f, :, base : base + LANES]
        tile = jnp.where(
            (lane80 >= rest) & (lane80 < rest + HALO),
            pltpu.roll(right_halo, (rest - 16 * f) % LANES, 1),
            tile,
        )
        tile = jnp.where(
            lane80 >= LANES - HALO,
            pltpu.roll(left_halo, (LANES - HALO - 16 * f) % LANES, 1),
            tile,
        )
        fields[f, :, base : base + LANES] = tile

    @pl.when(lat > 0)
    def _():
        high_leg.wait_recv()

    @pl.when(lat < n_lat - 1)
    def _():
        low_leg.wait_recv()

    both_leg = split(leg_halo[...].reshape(own * 2 * HALO, degrees))
    leg_high[inner_rows:, :], leg_low[inner_rows:, :] = both_leg

    values = jnp.zeros((16, leg_high.shape[0]), jnp.float32)
    lows = jnp.zeros((8, leg_high.shape[0]), jnp.float32)
    for dy in [0] + bands[::-1]:
        there = lax.rem(y + dy, n_y)
        if dy:
            pltpu.make_async_copy(c_out, c_in.at[there], c_recv.at[dy]).wait()
        block = pl.ds(pl.multiple_of(there * chunk, chunk), chunk)
        spectral = stacked((c_in[there] if dy else c_out[...]) * love_ref[:, block])
        values = values + dot(spectral, leg_high[:, block], ((1,), (1,)))
        lows = lows + dot(spectral[0:8], leg_low[:, block], ((1,), (1,)))
    values = values[0:8] + values[8:16] + lows
    body = jnp.zeros((8, LANES), jnp.float32)
    for h in range(inner_rows // LANES):
        body = body + jnp.where(
            wave8 == 2 * h + lane8 // rows, values[:, LANES * h : LANES * (h + 1)], 0.0
        )
    body = body + pltpu.roll(body, rows, 1)
    body = jnp.where(lane8 < rows, body, pltpu.roll(body, 4, 0))
    rim = jnp.concatenate(
        [values[:, inner_rows:], jnp.zeros((8, LANES - own * 2 * HALO), jnp.float32)], axis=1
    )
    rim = jnp.where(wave8 == lane8 // (2 * HALO), rim, 0.0)
    rim = jnp.where(row8 < 4, rim, pltpu.roll(rim, own * 2 * HALO, 1))
    rim = jnp.sum(rim, axis=0, keepdims=True)
    packet = jnp.where(row8 < 4, body, rim) * (1.0 / math.sqrt(count))
    d_out[...] = packet[0:5]
    for _, other in lons:
        lon_copy(3, d_out, d_in.at[lon], other).start()
    d_in[lon] = d_out[...]

    wet = fields[3]
    fields[1] = fields[1] * wet
    fields[2] = fields[2] * wet
    fields[3] = wet * STEP
    all_received(3, d_in, n_lon - 1)

    rows_kt = jnp.concatenate([d_in[:, m, :] for m in range(own)], axis=0)
    rows_tk = rows_kt.T
    rim_kt = jnp.concatenate(
        [d_in[:, 4, :], jnp.zeros((count - n_lon, LANES), jnp.float32)], axis=0
    )
    rim_tk = rim_kt.T
    rims = []
    for p in range(2):
        side = rim_tk[2 * HALO * own * p : 2 * HALO * (own * p + 1)]
        for m in range(1, own):
            first = 2 * HALO * (own * p + m)
            side = side + pltpu.roll(rim_tk[first : first + 2 * HALO], n_lon * m, 1)
        rims.append(side)
    coefficients = jnp.concatenate(
        [
            jnp.concatenate([rows_tk[0:rows], rows_tk[rows : 2 * rows]], axis=1),
            jnp.concatenate(rims, axis=1),
        ],
        axis=0,
    )
    coefficients = stacked(coefficients)
    loading = dot(coefficients, harm_high[...], ((1,), (0,)))
    loading = (
        loading[0:deep]
        + loading[deep : 2 * deep]
        + dot(coefficients[0:deep], harm_low[...], ((1,), (0,)))
    )

    pressure = fields[0] - loading
    east = fields[1]
    north = fields[2]
    step = fields[3]
    wide, tall = width - 1, deep - 1
    for _ in range(SUBSTEPS):
        east = east - step * (pltpu.roll(pressure, wide, 1) - pltpu.roll(pressure, 1, 1))
        north = north - step * (pltpu.roll(pressure, tall, 0) - pltpu.roll(pressure, 1, 0))
        pressure = pressure - step * (
            (pltpu.roll(east, wide, 1) - pltpu.roll(east, 1, 1))
            + (pltpu.roll(north, tall, 0) - pltpu.roll(north, 1, 0))
        )
    surface = pressure + loading
    loading_out[...] = loading[0:rows, 0:cols]
    surface_out[...] = surface[0:rows, 0:cols]
    east_out_ref[...] = east[0:rows, 0:cols]
    north_out_ref[...] = north[0:rows, 0:cols]

    all_sent(0, a_in, n_lon - 1)
    all_sent(1, b_in, n_lat - 1)
    for copy in c_copies:
        copy.wait_send()
    all_sent(3, d_in, n_lon - 1)
    left_copy.wait_send()
    right_copy.wait_send()

    @pl.when(lat > 0)
    def _():
        low_leg.wait_send()

    @pl.when(lat < n_lat - 1)
    def _():
        high_leg.wait_send()


def write_kernel(a_ref, b_ref, c_ref, d_ref, a_out, b_out, c_out, d_out, sem):
    pairs = ((a_ref, a_out), (b_ref, b_out), (c_ref, c_out), (d_ref, d_out))
    copies = [pltpu.make_async_copy(src, dst, sem.at[k]) for k, (src, dst) in enumerate(pairs)]
    for copy in copies:
        copy.start()
    for copy in copies:
        copy.wait()


def shards(height, east_flow, north_flow, legendre, love_numbers, wavenumbers, land_sea):
    n_lat, n_lon = lax.axis_size("lat"), lax.axis_size("lon")
    rows, cols = height.shape
    own, _, degrees = legendre.shape
    width = -(-(cols + 2 * HALO) // LANES) * LANES
    deep = rows + 2 * HALO
    chunk = degrees // (n_lat // 2)
    vmem = pl.BlockSpec(memory_space=pltpu.VMEM)
    f32 = jnp.float32
    shape = jax.ShapeDtypeStruct((rows, cols), f32)
    held = pltpu.VMEM((rows, cols), f32)
    results = pl.pallas_call(
        functools.partial(kernel, n_lat, n_lon),
        out_shape=(held, held, held, held),
        in_specs=[pl.BlockSpec(memory_space=pltpu.HBM)] * 7,
        out_specs=(vmem, vmem, vmem, vmem),
        scratch_shapes=[
            held,
            held,
            held,
            pltpu.VMEM((rows, cols), jnp.int32),
            pltpu.VMEM((1, degrees), f32),
            pltpu.VMEM((1, wavenumbers.shape[0]), jnp.int32),
            pltpu.VMEM((4, deep, width), f32),
            pltpu.VMEM((own * n_lon, LANES), f32),
            pltpu.VMEM((2 * own * n_lon, width), jnp.bfloat16),
            pltpu.VMEM((2 * own * n_lon, width), jnp.bfloat16),
            pltpu.VMEM((own, rows, degrees), f32),
            pltpu.VMEM((own * deep, degrees), jnp.bfloat16),
            pltpu.VMEM((own * deep, degrees), jnp.bfloat16),
            pltpu.VMEM((own, 2 * HALO, degrees), f32),
            pltpu.VMEM((n_lon, own, LANES), f32),
            pltpu.VMEM((n_lon, own, LANES), f32),
            pltpu.VMEM((n_lat // 2, 8, chunk), f32),
            pltpu.VMEM((n_lat, 8, chunk), f32),
            pltpu.VMEM((8, chunk), f32),
            pltpu.VMEM((n_lat // 2, 8, chunk), f32),
            pltpu.VMEM((5, LANES), f32),
            pltpu.VMEM((n_lon, 5, LANES), f32),
            pltpu.VMEM((deep, LANES), f32),
            pltpu.VMEM((deep, LANES), f32),
            pltpu.VMEM((deep, LANES), f32),
            pltpu.VMEM((deep, LANES), f32),
            pltpu.SemaphoreType.DMA((7,)),
            pltpu.SemaphoreType.DMA((4,)),
            pltpu.SemaphoreType.DMA((4,)),
            pltpu.SemaphoreType.DMA((6,)),
            pltpu.SemaphoreType.DMA((6,)),
            pltpu.SemaphoreType.DMA((n_lat // 2,)),
            pltpu.SemaphoreType.DMA((n_lat // 2,)),
        ],
        compiler_params=pltpu.CompilerParams(
            collective_id=0, has_side_effects=True, vmem_limit_bytes=24 << 20
        ),
    )(
        *[
            pltpu.with_memory_space_constraint(x, pltpu.HBM)
            for x in (
                height,
                east_flow,
                north_flow,
                land_sea,
                legendre,
                love_numbers.reshape(1, degrees),
                wavenumbers.reshape(1, wavenumbers.shape[0]),
            )
        ]
    )
    anywhere = pl.BlockSpec(memory_space=pl.ANY)
    return pl.pallas_call(
        write_kernel,
        out_shape=(shape, shape, shape, shape),
        in_specs=[vmem, vmem, vmem, vmem],
        out_specs=(anywhere, anywhere, anywhere, anywhere),
        scratch_shapes=[pltpu.SemaphoreType.DMA((4,))],
        compiler_params=pltpu.CompilerParams(vmem_limit_bytes=8 << 20),
    )(*results)


def solution(mesh):
    return jax.shard_map(
        shards,
        mesh=mesh,
        in_specs=(
            P("lat", "lon"),
            P("lat", "lon"),
            P("lat", "lon"),
            P("lon", "lat", None),
            P(),
            P(),
            P("lat", "lon"),
        ),
        out_specs=(P("lat", "lon"), P("lat", "lon"), P("lat", "lon"), P("lat", "lon")),
        check_vma=False,
    )
```

```python
import functools
import math

import jax
import jax.numpy as jnp
from jax import lax
from jax.experimental import pallas as pl
from jax.experimental.pallas import tpu as pltpu
from jax.sharding import PartitionSpec as P

SUBSTEPS = 4
HALO = 2 * SUBSTEPS
LANES = 128
STEP = 0.3
MESH = pl.DeviceIdType.MESH


def dot(a, b, dims):
    return lax.dot_general(a, b, (dims, ((), ())), preferred_element_type=jnp.float32)


def split(x):
    high = x.astype(jnp.bfloat16)
    return high, (x - high.astype(jnp.float32)).astype(jnp.bfloat16)


def stacked(x):
    return jnp.concatenate([x, x - x.astype(jnp.bfloat16).astype(jnp.float32)], axis=0).astype(
        jnp.bfloat16
    )


def hops(n, d):
    return min(d, n - d)


def lat_partners(n_lat, lat):
    n_y = n_lat // 2
    x_hi, y = lax.div(lat, n_y), lax.rem(lat, n_y)
    steps = [(2 * dx + hops(n_y, dy), dx, dy) for dx in range(2) for dy in range(n_y)]
    steps = sorted((step for step in steps if step[0]), reverse=True)
    return [
        (far, (1 - x_hi if dx else x_hi) * n_y + lax.rem(y + dy, n_y)) for far, dx, dy in steps
    ]


def lon_partners(n_lon, lon):
    n_z = n_lon // 4
    z, x_lo, core = lax.div(lon, 4), lax.rem(lax.div(lon, 2), 2), lax.rem(lon, 2)
    steps = [
        (hops(n_z, dz) + dx, dz, dx, dc)
        for dz in range(n_z)
        for dx in range(2)
        for dc in range(2)
        if dz or dx or dc
    ]
    return [
        (
            far,
            lax.rem(z + dz, n_z) * 4 + (1 - x_lo if dx else x_lo) * 2 + (1 - core if dc else core),
        )
        for far, dz, dx, dc in sorted(steps, reverse=True)
    ]


def kernel(
    n_lat,
    n_lon,
    height_hbm,
    east_hbm,
    north_hbm,
    land_hbm,
    legendre_ref,
    love_hbm,
    waves_hbm,
    loading_out,
    surface_out,
    east_out_ref,
    north_out_ref,
    height_ref,
    east_ref,
    north_ref,
    land_ref,
    love_ref,
    waves_ref,
    fields,
    steps,
    by_slot,
    harm_high,
    harm_low,
    leg_own,
    leg_high,
    leg_low,
    leg_halo,
    a_out,
    a_in,
    b_out,
    b_in,
    c_out,
    c_in,
    d_out,
    d_in,
    to_left,
    to_right,
    from_right,
    from_left,
    in_sem,
    send_sem,
    recv_sem,
    edge_send,
    edge_recv,
    c_send,
    c_recv,
):
    lat = lax.axis_index("lat")
    lon = lax.axis_index("lon")
    rows, cols = height_ref.shape
    own = legendre_ref.shape[0]
    width = fields.shape[2]
    period = cols * n_lon
    base, rest = cols // LANES * LANES, cols % LANES
    lats = lat_partners(n_lat, lat)
    lons = lon_partners(n_lon, lon)

    inputs = [
        pltpu.make_async_copy(src, dst, in_sem.at[k])
        for k, (src, dst) in enumerate(
            (
                (waves_hbm, waves_ref),
                (height_hbm, height_ref),
                (east_hbm, east_ref),
                (north_hbm, north_ref),
                (land_hbm, land_ref),
                (love_hbm, love_ref),
                (legendre_ref, leg_own),
            )
        )
    ]
    for copy in inputs:
        copy.start()
    barrier = pltpu.get_barrier_semaphore()
    everyone = [(far, (other, lon)) for far, other in lats]
    everyone += [(far, (lat, other)) for far, other in lons]
    for _, where in sorted(everyone, key=lambda other: -other[0]):
        pl.semaphore_signal(barrier, inc=1, device_id=where, device_id_type=MESH)
    n_y = n_lat // 2
    y = lax.rem(lat, n_y)
    for copy in inputs[:6]:
        copy.wait()

    for f, ref in enumerate((height_ref, east_ref, north_ref, land_ref)):
        fields[f, 0:rows, base:width] = jnp.zeros((rows, width - base), jnp.float32)
        fields[f, 0:rows, 0:cols] = ref[...].astype(jnp.float32)
    high, low = split(fields[0, 0:rows, :])
    twice_high = jnp.concatenate([high, high], axis=0)
    twice_low = jnp.concatenate([low, low], axis=0)

    count = waves_ref.shape[1]
    by_slot[...] = jnp.broadcast_to(waves_ref[...].astype(jnp.float32), (LANES, count)).T
    waves = jnp.concatenate([by_slot[pl.ds(m, n_lon, stride=own), :] for m in range(own)], axis=0)
    start = jnp.bitwise_and(waves.astype(jnp.int32) * lon, n_lon - 1).astype(jnp.float32) * cols
    quarter = period // 4
    lane = lax.broadcasted_iota(jnp.int32, (16, width), 1)
    column = jnp.where(lane < width - 64, lane, lane - width).astype(jnp.float32)
    for g in range(count // 16):
        here = slice(16 * g, 16 * g + 16)
        wave = jnp.concatenate([waves[here]] * (width // LANES), axis=1)
        first = jnp.concatenate([start[here]] * (width // LANES), axis=1)
        r = wave * column + first
        turn = (r * (1.0 / quarter) + 4096.5).astype(jnp.int32)
        d = r - (turn - 4096).astype(jnp.float32) * quarter
        phi = d * (2.0 * math.pi / period)
        s = phi * phi
        sin = 1.0 / 362880.0
        sin = sin * s - 1.0 / 5040.0
        sin = sin * s + 1.0 / 120.0
        sin = sin * s - 1.0 / 6.0
        sin = phi + phi * (s * sin)
        cos = -1.0 / 3628800.0
        cos = cos * s + 1.0 / 40320.0
        cos = cos * s - 1.0 / 720.0
        cos = cos * s + 1.0 / 24.0
        cos = cos * s - 0.5
        cos = 1.0 + s * cos
        odd = jnp.bitwise_and(turn, 1) == 1
        cos_minus = jnp.bitwise_and(turn + 1, 2) == 2
        sin_minus = jnp.bitwise_and(turn, 2) == 2
        c = jnp.where(odd, sin, cos)
        c = jnp.where(cos_minus, -c, c)
        n = jnp.where(odd, cos, sin)
        n = jnp.where(sin_minus, -n, n)
        there = slice(count + 16 * g, count + 16 * g + 16)
        harm_high[here, :], harm_low[here, :] = split(c)
        harm_high[there, :], harm_low[there, :] = split(n)

    partial = (
        dot(harm_high[...], twice_high, ((1,), (1,)))
        + dot(harm_high[...], twice_low, ((1,), (1,)))
        + dot(harm_low[...], twice_high, ((1,), (1,)))
    )
    half = lax.broadcasted_iota(jnp.int32, (count, LANES), 1) < rows
    partial = jnp.where(half, partial[0:count], partial[count : 2 * count])
    for m in range(own):
        a_out[:, m, :] = partial[n_lon * m : n_lon * (m + 1)]

    pl.semaphore_wait(barrier, n_lat + n_lon - 2)

    def lon_copy(k, src, dst, other):
        return pltpu.make_async_remote_copy(
            src_ref=src,
            dst_ref=dst,
            send_sem=send_sem.at[k],
            recv_sem=recv_sem.at[k],
            device_id=(lat, other),
            device_id_type=MESH,
        )

    def lat_copy(k, src, dst, other):
        return pltpu.make_async_remote_copy(
            src_ref=src,
            dst_ref=dst,
            send_sem=send_sem.at[k],
            recv_sem=recv_sem.at[k],
            device_id=(other, lon),
            device_id_type=MESH,
        )

    def all_received(k, ref, n):
        pltpu.make_async_copy(ref.at[pl.ds(0, n)], ref.at[pl.ds(0, n)], recv_sem.at[k]).wait()

    def all_sent(k, ref, n):
        pltpu.make_async_copy(ref.at[pl.ds(0, n)], ref.at[pl.ds(0, n)], send_sem.at[k]).wait()

    for _, other in lons:
        lon_copy(0, a_out.at[other], a_in.at[lon], other).start()
    a_in[lon] = a_out[lon]

    below, above = jnp.minimum(lat + 1, n_lat - 1), jnp.maximum(lat - 1, 0)

    def edge_copy(k, src, dst, where):
        return pltpu.make_async_remote_copy(
            src_ref=src,
            dst_ref=dst,
            send_sem=edge_send.at[k],
            recv_sem=edge_recv.at[k],
            device_id=where,
            device_id_type=MESH,
        )

    low_rows = edge_copy(
        0, fields.at[:, 0:HALO, :], fields.at[:, rows : rows + HALO, :], (above, lon)
    )
    high_rows = edge_copy(
        1,
        fields.at[:, rows - HALO : rows, :],
        fields.at[:, rows + HALO : rows + 2 * HALO, :],
        (below, lon),
    )
    low_leg = edge_copy(
        2, legendre_ref.at[:, 0:HALO, :], leg_halo.at[:, 0:HALO, :], (above, lon)
    )
    high_leg = edge_copy(
        3,
        legendre_ref.at[:, rows - HALO : rows, :],
        leg_halo.at[:, HALO : 2 * HALO, :],
        (below, lon),
    )

    @pl.when(lat > 0)
    def _():
        low_rows.start()
        low_leg.start()

    @pl.when(lat < n_lat - 1)
    def _():
        high_rows.start()
        high_leg.start()

    @pl.when(lat == 0)
    def _():
        fields[:, rows + HALO : rows + 2 * HALO, :] = jnp.zeros((4, HALO, width), jnp.float32)
        leg_halo[:, HALO : 2 * HALO, :] = jnp.zeros((own, HALO, leg_halo.shape[2]), jnp.float32)

    @pl.when(lat == n_lat - 1)
    def _():
        fields[:, rows : rows + HALO, :] = jnp.zeros((4, HALO, width), jnp.float32)
        leg_halo[:, 0:HALO, :] = jnp.zeros((own, HALO, leg_halo.shape[2]), jnp.float32)

    inputs[6].wait()
    inner_rows = own * rows
    for m in range(own):
        here = slice(rows * m, rows * (m + 1))
        leg_high[here, :], leg_low[here, :] = split(leg_own[m])
    all_received(0, a_in, n_lon - 1)
    fourier = jnp.sum(a_in[...], axis=0) * (1.0 / math.sqrt(period))

    degrees = leg_own.shape[2]
    lane8 = lax.broadcasted_iota(jnp.int32, (8, LANES), 1)
    row8 = lax.broadcasted_iota(jnp.int32, (8, LANES), 0)
    both = jnp.concatenate([fourier, fourier], axis=0)
    swapped = pltpu.roll(both, rows, 1)
    spread = jnp.where((lane8 < rows) == (row8 < 4), both, swapped)
    wave8 = jnp.bitwise_and(row8, 3)
    left = jnp.concatenate(
        [jnp.where(wave8 == 2 * h + lane8 // rows, spread, 0.0) for h in range(own * rows // LANES)],
        axis=1,
    )
    left = stacked(left)
    chunk = degrees // n_y
    bands = sorted(range(1, n_y), key=lambda dy: -hops(n_y, dy))
    for slot, dy in enumerate(bands + [0]):
        there = lax.rem(y + dy, n_y)
        block = pl.ds(pl.multiple_of(there * chunk, chunk), chunk)
        part = dot(left, leg_high[0:inner_rows, block], ((1,), (0,)))
        part = part[0:8] + part[8:16] + dot(left[0:8], leg_low[0:inner_rows, block], ((1,), (0,)))
        b_out[slot] = part
        lat_copy(1, b_out.at[slot], b_in.at[lat], n_lat - n_y - (lat - y) + there).start()
        if dy:
            lat_copy(1, b_out.at[slot], b_in.at[lat], lat - y + there).start()
        else:
            b_in[lat] = part

    @pl.when(lat > 0)
    def _():
        high_rows.wait_recv()

    @pl.when(lat < n_lat - 1)
    def _():
        low_rows.wait_recv()

    deep = fields.shape[1]
    lane80 = lax.broadcasted_iota(jnp.int32, (deep, LANES), 1)
    packed_left = jnp.zeros((deep, LANES), jnp.float32)
    packed_right = jnp.zeros((deep, LANES), jnp.float32)
    for f in range(4):
        here = (lane80 >= 16 * f) & (lane80 < 16 * f + HALO)
        west = fields[f, :, 0:LANES]
        east = fields[f, :, base : base + LANES]
        packed_left = jnp.where(here, pltpu.roll(west, 16 * f, 1), packed_left)
        packed_right = jnp.where(
            here, pltpu.roll(east, (16 * f - (rest - HALO)) % LANES, 1), packed_right
        )
    to_left[...] = packed_left
    to_right[...] = packed_right
    west_side, east_side = lax.rem(lon + n_lon - 1, n_lon), lax.rem(lon + 1, n_lon)
    left_copy = edge_copy(4, to_left, from_right, (lat, west_side))
    right_copy = edge_copy(5, to_right, from_left, (lat, east_side))
    left_copy.start()
    right_copy.start()

    all_received(1, b_in, n_lat - 1)

    c_out[...] = jnp.sum(b_in[...], axis=0)
    c_copies = [
        pltpu.make_async_remote_copy(
            src_ref=c_out,
            dst_ref=c_in.at[y],
            send_sem=c_send.at[dy],
            recv_sem=c_recv.at[n_y - dy],
            device_id=(lat - y + lax.rem(y + dy, n_y), lon),
            device_id_type=MESH,
        )
        for dy in bands
    ]
    for copy in c_copies:
        copy.start()

    @pl.when(lat > 0)
    def _():
        low_rows.wait_send()

    @pl.when(lat < n_lat - 1)
    def _():
        high_rows.wait_send()

    left_copy.wait_recv()
    right_copy.wait_recv()
    right_halo = from_right[...]
    left_halo = from_left[...]
    for f in range(4):
        tile = fields[f, :, base : base + LANES]
        tile = jnp.where(
            (lane80 >= rest) & (lane80 < rest + HALO),
            pltpu.roll(right_halo, (rest - 16 * f) % LANES, 1),
            tile,
        )
        tile = jnp.where(
            lane80 >= LANES - HALO,
            pltpu.roll(left_halo, (LANES - HALO - 16 * f) % LANES, 1),
            tile,
        )
        fields[f, :, base : base + LANES] = tile

    @pl.when(lat > 0)
    def _():
        high_leg.wait_recv()

    @pl.when(lat < n_lat - 1)
    def _():
        low_leg.wait_recv()

    both_leg = split(leg_halo[...].reshape(own * 2 * HALO, degrees))
    leg_high[inner_rows:, :], leg_low[inner_rows:, :] = both_leg

    values = jnp.zeros((16, leg_high.shape[0]), jnp.float32)
    lows = jnp.zeros((8, leg_high.shape[0]), jnp.float32)
    for dy in [0] + bands[::-1]:
        there = lax.rem(y + dy, n_y)
        if dy:
            pltpu.make_async_copy(c_out, c_in.at[there], c_recv.at[dy]).wait()
        block = pl.ds(pl.multiple_of(there * chunk, chunk), chunk)
        spectral = stacked((c_in[there] if dy else c_out[...]) * love_ref[:, block])
        values = values + dot(spectral, leg_high[:, block], ((1,), (1,)))
        lows = lows + dot(spectral[0:8], leg_low[:, block], ((1,), (1,)))
    values = values[0:8] + values[8:16] + lows
    body = jnp.zeros((8, LANES), jnp.float32)
    for h in range(inner_rows // LANES):
        body = body + jnp.where(
            wave8 == 2 * h + lane8 // rows, values[:, LANES * h : LANES * (h + 1)], 0.0
        )
    body = body + pltpu.roll(body, rows, 1)
    body = jnp.where(lane8 < rows, body, pltpu.roll(body, 4, 0))
    rim = jnp.concatenate(
        [values[:, inner_rows:], jnp.zeros((8, LANES - own * 2 * HALO), jnp.float32)], axis=1
    )
    rim = jnp.where(wave8 == lane8 // (2 * HALO), rim, 0.0)
    rim = jnp.where(row8 < 4, rim, pltpu.roll(rim, own * 2 * HALO, 1))
    rim = jnp.sum(rim, axis=0, keepdims=True)
    packet = jnp.where(row8 < 4, body, rim) * (1.0 / math.sqrt(count))
    d_out[...] = packet[0:5]
    for _, other in lons:
        lon_copy(3, d_out, d_in.at[lon], other).start()
    d_in[lon] = d_out[...]

    wide, tall = width - 1, deep - 1
    wet = fields[3]
    step = wet * STEP
    fields[1] = pltpu.roll(fields[1] * wet, wide, 1)
    fields[2] = pltpu.roll(fields[2] * wet, tall, 0)
    fields[3] = step
    steps[0] = pltpu.roll(step, wide, 1)
    steps[1] = pltpu.roll(step, tall, 0)
    all_received(3, d_in, n_lon - 1)

    rows_kt = jnp.concatenate([d_in[:, m, :] for m in range(own)], axis=0)
    rows_tk = rows_kt.T
    rim_kt = jnp.concatenate(
        [d_in[:, 4, :], jnp.zeros((count - n_lon, LANES), jnp.float32)], axis=0
    )
    rim_tk = rim_kt.T
    rims = []
    for p in range(2):
        side = rim_tk[2 * HALO * own * p : 2 * HALO * (own * p + 1)]
        for m in range(1, own):
            first = 2 * HALO * (own * p + m)
            side = side + pltpu.roll(rim_tk[first : first + 2 * HALO], n_lon * m, 1)
        rims.append(side)
    coefficients = jnp.concatenate(
        [
            jnp.concatenate([rows_tk[0:rows], rows_tk[rows : 2 * rows]], axis=1),
            jnp.concatenate(rims, axis=1),
        ],
        axis=0,
    )
    coefficients = stacked(coefficients)
    loading = dot(coefficients, harm_high[...], ((1,), (0,)))
    loading = (
        loading[0:deep]
        + loading[deep : 2 * deep]
        + dot(coefficients[0:deep], harm_low[...], ((1,), (0,)))
    )

    pressure = fields[0] - loading
    east = fields[1]
    north = fields[2]
    step = fields[3]
    for _ in range(SUBSTEPS):
        east = east - steps[0] * (pltpu.roll(pressure, wide - 1, 1) - pressure)
        north = north - steps[1] * (pltpu.roll(pressure, tall - 1, 0) - pressure)
        pressure = pressure - step * (
            (east - pltpu.roll(east, 2, 1)) + (north - pltpu.roll(north, 2, 0))
        )
    east = pltpu.roll(east, 1, 1)
    north = pltpu.roll(north, 1, 0)
    surface = pressure + loading
    loading_out[...] = loading[0:rows, 0:cols]
    surface_out[...] = surface[0:rows, 0:cols]
    east_out_ref[...] = east[0:rows, 0:cols]
    north_out_ref[...] = north[0:rows, 0:cols]

    all_sent(0, a_in, n_lon - 1)
    all_sent(1, b_in, n_lat - 1)
    for copy in c_copies:
        copy.wait_send()
    all_sent(3, d_in, n_lon - 1)
    left_copy.wait_send()
    right_copy.wait_send()

    @pl.when(lat > 0)
    def _():
        low_leg.wait_send()

    @pl.when(lat < n_lat - 1)
    def _():
        high_leg.wait_send()


def write_kernel(a_ref, b_ref, c_ref, d_ref, a_out, b_out, c_out, d_out, sem):
    pairs = ((a_ref, a_out), (b_ref, b_out), (c_ref, c_out), (d_ref, d_out))
    copies = [pltpu.make_async_copy(src, dst, sem.at[k]) for k, (src, dst) in enumerate(pairs)]
    for copy in copies:
        copy.start()
    for copy in copies:
        copy.wait()


def shards(height, east_flow, north_flow, legendre, love_numbers, wavenumbers, land_sea):
    n_lat, n_lon = lax.axis_size("lat"), lax.axis_size("lon")
    rows, cols = height.shape
    own, _, degrees = legendre.shape
    width = -(-(cols + 2 * HALO) // LANES) * LANES
    deep = rows + 2 * HALO
    chunk = degrees // (n_lat // 2)
    vmem = pl.BlockSpec(memory_space=pltpu.VMEM)
    f32 = jnp.float32
    shape = jax.ShapeDtypeStruct((rows, cols), f32)
    held = pltpu.VMEM((rows, cols), f32)
    results = pl.pallas_call(
        functools.partial(kernel, n_lat, n_lon),
        out_shape=(held, held, held, held),
        in_specs=[pl.BlockSpec(memory_space=pltpu.HBM)] * 7,
        out_specs=(vmem, vmem, vmem, vmem),
        scratch_shapes=[
            held,
            held,
            held,
            pltpu.VMEM((rows, cols), jnp.int32),
            pltpu.VMEM((1, degrees), f32),
            pltpu.VMEM((1, wavenumbers.shape[0]), jnp.int32),
            pltpu.VMEM((4, deep, width), f32),
            pltpu.VMEM((2, deep, width), f32),
            pltpu.VMEM((own * n_lon, LANES), f32),
            pltpu.VMEM((2 * own * n_lon, width), jnp.bfloat16),
            pltpu.VMEM((2 * own * n_lon, width), jnp.bfloat16),
            pltpu.VMEM((own, rows, degrees), f32),
            pltpu.VMEM((own * deep, degrees), jnp.bfloat16),
            pltpu.VMEM((own * deep, degrees), jnp.bfloat16),
            pltpu.VMEM((own, 2 * HALO, degrees), f32),
            pltpu.VMEM((n_lon, own, LANES), f32),
            pltpu.VMEM((n_lon, own, LANES), f32),
            pltpu.VMEM((n_lat // 2, 8, chunk), f32),
            pltpu.VMEM((n_lat, 8, chunk), f32),
            pltpu.VMEM((8, chunk), f32),
            pltpu.VMEM((n_lat // 2, 8, chunk), f32),
            pltpu.VMEM((5, LANES), f32),
            pltpu.VMEM((n_lon, 5, LANES), f32),
            pltpu.VMEM((deep, LANES), f32),
            pltpu.VMEM((deep, LANES), f32),
            pltpu.VMEM((deep, LANES), f32),
            pltpu.VMEM((deep, LANES), f32),
            pltpu.SemaphoreType.DMA((7,)),
            pltpu.SemaphoreType.DMA((4,)),
            pltpu.SemaphoreType.DMA((4,)),
            pltpu.SemaphoreType.DMA((6,)),
            pltpu.SemaphoreType.DMA((6,)),
            pltpu.SemaphoreType.DMA((n_lat // 2,)),
            pltpu.SemaphoreType.DMA((n_lat // 2,)),
        ],
        compiler_params=pltpu.CompilerParams(
            collective_id=0, has_side_effects=True, vmem_limit_bytes=24 << 20
        ),
    )(
        *[
            pltpu.with_memory_space_constraint(x, pltpu.HBM)
            for x in (
                height,
                east_flow,
                north_flow,
                land_sea,
                legendre,
                love_numbers.reshape(1, degrees),
                wavenumbers.reshape(1, wavenumbers.shape[0]),
            )
        ]
    )
    anywhere = pl.BlockSpec(memory_space=pl.ANY)
    return pl.pallas_call(
        write_kernel,
        out_shape=(shape, shape, shape, shape),
        in_specs=[vmem, vmem, vmem, vmem],
        out_specs=(anywhere, anywhere, anywhere, anywhere),
        scratch_shapes=[pltpu.SemaphoreType.DMA((4,))],
        compiler_params=pltpu.CompilerParams(vmem_limit_bytes=8 << 20),
    )(*results)


def solution(mesh):
    return jax.shard_map(
        shards,
        mesh=mesh,
        in_specs=(
            P("lat", "lon"),
            P("lat", "lon"),
            P("lat", "lon"),
            P("lon", "lat", None),
            P(),
            P(),
            P("lat", "lon"),
        ),
        out_specs=(P("lat", "lon"), P("lat", "lon"), P("lat", "lon"), P("lat", "lon")),
        check_vma=False,
    )
```

```python
import functools
import math

import jax
import jax.numpy as jnp
from jax import lax
from jax.experimental import pallas as pl
from jax.experimental.pallas import tpu as pltpu
from jax.sharding import PartitionSpec as P

SUBSTEPS = 4
HALO = 2 * SUBSTEPS
LANES = 128
STEP = 0.3
MESH = pl.DeviceIdType.MESH


def dot(a, b, dims):
    return lax.dot_general(a, b, (dims, ((), ())), preferred_element_type=jnp.float32)


def split(x):
    high = x.astype(jnp.bfloat16)
    return high, (x - high.astype(jnp.float32)).astype(jnp.bfloat16)


def stacked(x):
    return jnp.concatenate([x, x - x.astype(jnp.bfloat16).astype(jnp.float32)], axis=0).astype(
        jnp.bfloat16
    )


def hops(n, d):
    return min(d, n - d)


def lat_partners(n_lat, lat):
    n_y = n_lat // 2
    x_hi, y = lax.div(lat, n_y), lax.rem(lat, n_y)
    steps = [(2 * dx + hops(n_y, dy), dx, dy) for dx in range(2) for dy in range(n_y)]
    steps = sorted((step for step in steps if step[0]), reverse=True)
    return [
        (far, (1 - x_hi if dx else x_hi) * n_y + lax.rem(y + dy, n_y)) for far, dx, dy in steps
    ]


def lon_partners(n_lon, lon):
    n_z = n_lon // 4
    z, x_lo, core = lax.div(lon, 4), lax.rem(lax.div(lon, 2), 2), lax.rem(lon, 2)
    steps = [
        (hops(n_z, dz) + dx, dz, dx, dc)
        for dz in range(n_z)
        for dx in range(2)
        for dc in range(2)
        if dz or dx or dc
    ]
    return [
        (
            far,
            lax.rem(z + dz, n_z) * 4 + (1 - x_lo if dx else x_lo) * 2 + (1 - core if dc else core),
        )
        for far, dz, dx, dc in sorted(steps, reverse=True)
    ]


def kernel(
    n_lat,
    n_lon,
    height_hbm,
    east_hbm,
    north_hbm,
    land_hbm,
    legendre_ref,
    love_hbm,
    waves_hbm,
    loading_out,
    surface_out,
    east_out_ref,
    north_out_ref,
    height_ref,
    east_ref,
    north_ref,
    land_ref,
    love_ref,
    waves_ref,
    fields,
    steps,
    by_slot,
    harm_high,
    harm_low,
    leg_own,
    leg_high,
    leg_low,
    leg_halo,
    a_out,
    a_in,
    b_out,
    b_in,
    c_out,
    c_in,
    d_out,
    d_in,
    to_left,
    to_right,
    from_right,
    from_left,
    in_sem,
    send_sem,
    recv_sem,
    edge_send,
    edge_recv,
    c_send,
    c_recv,
    d_send,
    d_recv,
):
    lat = lax.axis_index("lat")
    lon = lax.axis_index("lon")
    rows, cols = height_ref.shape
    own = legendre_ref.shape[0]
    width = fields.shape[2]
    period = cols * n_lon
    base, rest = cols // LANES * LANES, cols % LANES
    lats = lat_partners(n_lat, lat)
    lons = lon_partners(n_lon, lon)

    inputs = [
        pltpu.make_async_copy(src, dst, in_sem.at[k])
        for k, (src, dst) in enumerate(
            (
                (waves_hbm, waves_ref),
                (height_hbm, height_ref),
                (east_hbm, east_ref),
                (north_hbm, north_ref),
                (land_hbm, land_ref),
                (love_hbm, love_ref),
                (legendre_ref, leg_own),
            )
        )
    ]
    for copy in inputs:
        copy.start()
    barrier = pltpu.get_barrier_semaphore()
    everyone = [(far, (other, lon)) for far, other in lats]
    everyone += [(far, (lat, other)) for far, other in lons]
    for _, where in sorted(everyone, key=lambda other: -other[0]):
        pl.semaphore_signal(barrier, inc=1, device_id=where, device_id_type=MESH)
    n_y = n_lat // 2
    y = lax.rem(lat, n_y)
    for copy in inputs[:6]:
        copy.wait()

    for f, ref in enumerate((height_ref, east_ref, north_ref, land_ref)):
        fields[f, 0:rows, base:width] = jnp.zeros((rows, width - base), jnp.float32)
        fields[f, 0:rows, 0:cols] = ref[...].astype(jnp.float32)
    high, low = split(fields[0, 0:rows, :])
    twice_high = jnp.concatenate([high, high], axis=0)
    twice_low = jnp.concatenate([low, low], axis=0)

    count = waves_ref.shape[1]
    by_slot[...] = jnp.broadcast_to(waves_ref[...].astype(jnp.float32), (LANES, count)).T
    chips = n_lon // 2
    waves = jnp.concatenate(
        [
            by_slot[pl.ds(own * c + m, chips, stride=2 * own), :]
            for m in range(own)
            for c in range(2)
        ],
        axis=0,
    )

    def slot_of(device):
        return lax.rem(device, 2) * chips + lax.div(device, 2)

    start = jnp.bitwise_and(waves.astype(jnp.int32) * lon, n_lon - 1).astype(jnp.float32) * cols
    quarter = period // 4
    lane = lax.broadcasted_iota(jnp.int32, (16, width), 1)
    column = jnp.where(lane < width - 64, lane, lane - width).astype(jnp.float32)
    for g in range(count // 16):
        here = slice(16 * g, 16 * g + 16)
        wave = jnp.concatenate([waves[here]] * (width // LANES), axis=1)
        first = jnp.concatenate([start[here]] * (width // LANES), axis=1)
        r = wave * column + first
        turn = (r * (1.0 / quarter) + 4096.5).astype(jnp.int32)
        d = r - (turn - 4096).astype(jnp.float32) * quarter
        phi = d * (2.0 * math.pi / period)
        s = phi * phi
        sin = 1.0 / 362880.0
        sin = sin * s - 1.0 / 5040.0
        sin = sin * s + 1.0 / 120.0
        sin = sin * s - 1.0 / 6.0
        sin = phi + phi * (s * sin)
        cos = -1.0 / 3628800.0
        cos = cos * s + 1.0 / 40320.0
        cos = cos * s - 1.0 / 720.0
        cos = cos * s + 1.0 / 24.0
        cos = cos * s - 0.5
        cos = 1.0 + s * cos
        odd = jnp.bitwise_and(turn, 1) == 1
        cos_minus = jnp.bitwise_and(turn + 1, 2) == 2
        sin_minus = jnp.bitwise_and(turn, 2) == 2
        c = jnp.where(odd, sin, cos)
        c = jnp.where(cos_minus, -c, c)
        n = jnp.where(odd, cos, sin)
        n = jnp.where(sin_minus, -n, n)
        there = slice(count + 16 * g, count + 16 * g + 16)
        harm_high[here, :], harm_low[here, :] = split(c)
        harm_high[there, :], harm_low[there, :] = split(n)

    partial = (
        dot(harm_high[...], twice_high, ((1,), (1,)))
        + dot(harm_high[...], twice_low, ((1,), (1,)))
        + dot(harm_low[...], twice_high, ((1,), (1,)))
    )
    half = lax.broadcasted_iota(jnp.int32, (count, LANES), 1) < rows
    partial = jnp.where(half, partial[0:count], partial[count : 2 * count])
    for m in range(own):
        a_out[:, m, :] = partial[n_lon * m : n_lon * (m + 1)]

    pl.semaphore_wait(barrier, n_lat + n_lon - 2)

    def lon_copy(k, src, dst, other):
        return pltpu.make_async_remote_copy(
            src_ref=src,
            dst_ref=dst,
            send_sem=send_sem.at[k],
            recv_sem=recv_sem.at[k],
            device_id=(lat, other),
            device_id_type=MESH,
        )

    def lat_copy(k, src, dst, other):
        return pltpu.make_async_remote_copy(
            src_ref=src,
            dst_ref=dst,
            send_sem=send_sem.at[k],
            recv_sem=recv_sem.at[k],
            device_id=(other, lon),
            device_id_type=MESH,
        )

    def all_received(k, ref, n):
        pltpu.make_async_copy(ref.at[pl.ds(0, n)], ref.at[pl.ds(0, n)], recv_sem.at[k]).wait()

    def all_sent(k, ref, n):
        pltpu.make_async_copy(ref.at[pl.ds(0, n)], ref.at[pl.ds(0, n)], send_sem.at[k]).wait()

    for _, other in lons:
        lon_copy(0, a_out.at[slot_of(other)], a_in.at[lon], other).start()
    a_in[lon] = a_out[slot_of(lon)]

    below, above = jnp.minimum(lat + 1, n_lat - 1), jnp.maximum(lat - 1, 0)

    def edge_copy(k, src, dst, where):
        return pltpu.make_async_remote_copy(
            src_ref=src,
            dst_ref=dst,
            send_sem=edge_send.at[k],
            recv_sem=edge_recv.at[k],
            device_id=where,
            device_id_type=MESH,
        )

    low_rows = edge_copy(
        0, fields.at[:, 0:HALO, :], fields.at[:, rows : rows + HALO, :], (above, lon)
    )
    high_rows = edge_copy(
        1,
        fields.at[:, rows - HALO : rows, :],
        fields.at[:, rows + HALO : rows + 2 * HALO, :],
        (below, lon),
    )
    low_leg = edge_copy(
        2, legendre_ref.at[:, 0:HALO, :], leg_halo.at[:, 0:HALO, :], (above, lon)
    )
    high_leg = edge_copy(
        3,
        legendre_ref.at[:, rows - HALO : rows, :],
        leg_halo.at[:, HALO : 2 * HALO, :],
        (below, lon),
    )

    @pl.when(lat > 0)
    def _():
        low_rows.start()
        low_leg.start()

    @pl.when(lat < n_lat - 1)
    def _():
        high_rows.start()
        high_leg.start()

    @pl.when(lat == 0)
    def _():
        fields[:, rows + HALO : rows + 2 * HALO, :] = jnp.zeros((4, HALO, width), jnp.float32)
        leg_halo[:, HALO : 2 * HALO, :] = jnp.zeros((own, HALO, leg_halo.shape[2]), jnp.float32)

    @pl.when(lat == n_lat - 1)
    def _():
        fields[:, rows : rows + HALO, :] = jnp.zeros((4, HALO, width), jnp.float32)
        leg_halo[:, 0:HALO, :] = jnp.zeros((own, HALO, leg_halo.shape[2]), jnp.float32)

    inputs[6].wait()
    inner_rows = own * rows
    for m in range(own):
        here = slice(rows * m, rows * (m + 1))
        leg_high[here, :], leg_low[here, :] = split(leg_own[m])
    all_received(0, a_in, n_lon - 1)
    fourier = jnp.sum(a_in[...], axis=0) * (1.0 / math.sqrt(period))

    degrees = leg_own.shape[2]
    lane8 = lax.broadcasted_iota(jnp.int32, (8, LANES), 1)
    row8 = lax.broadcasted_iota(jnp.int32, (8, LANES), 0)
    both = jnp.concatenate([fourier, fourier], axis=0)
    swapped = pltpu.roll(both, rows, 1)
    spread = jnp.where((lane8 < rows) == (row8 < 4), both, swapped)
    wave8 = jnp.bitwise_and(row8, 3)
    left = jnp.concatenate(
        [jnp.where(wave8 == 2 * h + lane8 // rows, spread, 0.0) for h in range(own * rows // LANES)],
        axis=1,
    )
    left = stacked(left)
    chunk = degrees // n_y
    bands = sorted(range(1, n_y), key=lambda dy: -hops(n_y, dy))
    for slot, dy in enumerate(bands + [0]):
        there = lax.rem(y + dy, n_y)
        block = pl.ds(pl.multiple_of(there * chunk, chunk), chunk)
        part = dot(left, leg_high[0:inner_rows, block], ((1,), (0,)))
        part = part[0:8] + part[8:16] + dot(left[0:8], leg_low[0:inner_rows, block], ((1,), (0,)))
        b_out[slot] = part
        lat_copy(1, b_out.at[slot], b_in.at[lat], n_lat - n_y - (lat - y) + there).start()
        if dy:
            lat_copy(1, b_out.at[slot], b_in.at[lat], lat - y + there).start()
        else:
            b_in[lat] = part

    @pl.when(lat > 0)
    def _():
        high_rows.wait_recv()

    @pl.when(lat < n_lat - 1)
    def _():
        low_rows.wait_recv()

    deep = fields.shape[1]
    lane80 = lax.broadcasted_iota(jnp.int32, (deep, LANES), 1)
    packed_left = jnp.zeros((deep, LANES), jnp.float32)
    packed_right = jnp.zeros((deep, LANES), jnp.float32)
    for f in range(4):
        here = (lane80 >= 16 * f) & (lane80 < 16 * f + HALO)
        west = fields[f, :, 0:LANES]
        east = fields[f, :, base : base + LANES]
        packed_left = jnp.where(here, pltpu.roll(west, 16 * f, 1), packed_left)
        packed_right = jnp.where(
            here, pltpu.roll(east, (16 * f - (rest - HALO)) % LANES, 1), packed_right
        )
    to_left[...] = packed_left
    to_right[...] = packed_right
    west_side, east_side = lax.rem(lon + n_lon - 1, n_lon), lax.rem(lon + 1, n_lon)
    left_copy = edge_copy(4, to_left, from_right, (lat, west_side))
    right_copy = edge_copy(5, to_right, from_left, (lat, east_side))
    left_copy.start()
    right_copy.start()

    all_received(1, b_in, n_lat - 1)

    c_out[...] = jnp.sum(b_in[...], axis=0)
    c_copies = [
        pltpu.make_async_remote_copy(
            src_ref=c_out,
            dst_ref=c_in.at[y],
            send_sem=c_send.at[dy],
            recv_sem=c_recv.at[n_y - dy],
            device_id=(lat - y + lax.rem(y + dy, n_y), lon),
            device_id_type=MESH,
        )
        for dy in bands
    ]
    for copy in c_copies:
        copy.start()

    @pl.when(lat > 0)
    def _():
        low_rows.wait_send()

    @pl.when(lat < n_lat - 1)
    def _():
        high_rows.wait_send()

    left_copy.wait_recv()
    right_copy.wait_recv()
    right_halo = from_right[...]
    left_halo = from_left[...]
    for f in range(4):
        tile = fields[f, :, base : base + LANES]
        tile = jnp.where(
            (lane80 >= rest) & (lane80 < rest + HALO),
            pltpu.roll(right_halo, (rest - 16 * f) % LANES, 1),
            tile,
        )
        tile = jnp.where(
            lane80 >= LANES - HALO,
            pltpu.roll(left_halo, (LANES - HALO - 16 * f) % LANES, 1),
            tile,
        )
        fields[f, :, base : base + LANES] = tile

    @pl.when(lat > 0)
    def _():
        high_leg.wait_recv()

    @pl.when(lat < n_lat - 1)
    def _():
        low_leg.wait_recv()

    both_leg = split(leg_halo[...].reshape(own * 2 * HALO, degrees))
    leg_high[inner_rows:, :], leg_low[inner_rows:, :] = both_leg

    values = jnp.zeros((16, leg_high.shape[0]), jnp.float32)
    lows = jnp.zeros((8, leg_high.shape[0]), jnp.float32)
    for dy in [0] + bands[::-1]:
        there = lax.rem(y + dy, n_y)
        if dy:
            pltpu.make_async_copy(c_out, c_in.at[there], c_recv.at[dy]).wait()
        block = pl.ds(pl.multiple_of(there * chunk, chunk), chunk)
        spectral = stacked((c_in[there] if dy else c_out[...]) * love_ref[:, block])
        values = values + dot(spectral, leg_high[:, block], ((1,), (1,)))
        lows = lows + dot(spectral[0:8], leg_low[:, block], ((1,), (1,)))
    values = values[0:8] + values[8:16] + lows
    body = jnp.zeros((8, LANES), jnp.float32)
    for h in range(inner_rows // LANES):
        body = body + jnp.where(
            wave8 == 2 * h + lane8 // rows, values[:, LANES * h : LANES * (h + 1)], 0.0
        )
    body = body + pltpu.roll(body, rows, 1)
    body = jnp.where(lane8 < rows, body, pltpu.roll(body, 4, 0))
    rim = jnp.concatenate(
        [values[:, inner_rows:], jnp.zeros((8, LANES - own * 2 * HALO), jnp.float32)], axis=1
    )
    rim = jnp.where(wave8 == lane8 // (2 * HALO), rim, 0.0)
    rim = jnp.where(row8 < 4, rim, pltpu.roll(rim, own * 2 * HALO, 1))
    rim = jnp.sum(rim, axis=0, keepdims=True)
    packet = jnp.where(row8 < 4, body, rim) * (1.0 / math.sqrt(count))
    d_out[...] = packet[0:5]
    n_z = n_lon // 4
    z, x_lo, core = lax.div(lon, 4), lax.rem(lax.div(lon, 2), 2), lax.rem(lon, 2)
    mine = slot_of(lon)

    def packet_copy(src, slots, k, other):
        return pltpu.make_async_remote_copy(
            src_ref=src,
            dst_ref=d_in.at[slots],
            send_sem=d_send.at[k],
            recv_sem=d_recv.at[k],
            device_id=(lat, other),
            device_id_type=MESH,
        )

    def packets(count):
        return d_in.at[pl.ds(0, count)]

    far = n_z // 2
    near = sorted((dz for dz in range(n_z) if dz != far), key=lambda dz: hops(n_z, dz))
    for dx, dc in ((1, 1), (1, 0), (0, 1), (0, 0)):
        other = lax.rem(z + far, n_z) * 4
        other = other + (1 - x_lo if dx else x_lo) * 2 + (1 - core if dc else core)
        packet_copy(d_out, mine, far, other).start()
    for dz in near[::-1]:
        for dx in (1, 0):
            if dz or dx:
                other = lax.rem(z + dz, n_z) * 4 + (1 - x_lo if dx else x_lo) * 2 + core
                pltpu.make_async_remote_copy(
                    src_ref=d_out,
                    dst_ref=d_in.at[mine],
                    send_sem=d_send.at[far],
                    recv_sem=d_recv.at[(n_z - dz) % n_z],
                    device_id=(lat, other),
                    device_id_type=MESH,
                ).start()
    d_in[mine] = d_out[...]

    wide, tall = width - 1, deep - 1
    wet = fields[3]
    step = wet * STEP
    fields[1] = pltpu.roll(fields[1] * wet, wide, 1)
    fields[2] = pltpu.roll(fields[2] * wet, tall, 0)
    fields[3] = step
    steps[0] = pltpu.roll(step, wide, 1)
    steps[1] = pltpu.roll(step, tall, 0)

    for dz in near:
        count_in = 2 if dz else 1
        pltpu.make_async_copy(packets(count_in), packets(count_in), d_recv.at[dz]).wait()
        pair = pl.ds(core * chips + 2 * lax.rem(z + dz, n_z), 2)
        packet_copy(d_in.at[pair], pair, n_z, lon + 1 - 2 * core).start()
    handed = 2 * len(near)
    pltpu.make_async_copy(packets(handed), packets(handed), d_recv.at[n_z]).wait()
    pltpu.make_async_copy(packets(4), packets(4), d_recv.at[far]).wait()

    rows_kt = jnp.concatenate([d_in[:, m, :] for m in range(own)], axis=0)
    rows_tk = rows_kt.T
    rim_kt = jnp.concatenate(
        [d_in[:, 4, :], jnp.zeros((count - n_lon, LANES), jnp.float32)], axis=0
    )
    rim_tk = rim_kt.T
    rims = []
    for p in range(2):
        side = rim_tk[2 * HALO * own * p : 2 * HALO * (own * p + 1)]
        for m in range(1, own):
            first = 2 * HALO * (own * p + m)
            side = side + pltpu.roll(rim_tk[first : first + 2 * HALO], n_lon * m, 1)
        rims.append(side)
    coefficients = jnp.concatenate(
        [
            jnp.concatenate([rows_tk[0:rows], rows_tk[rows : 2 * rows]], axis=1),
            jnp.concatenate(rims, axis=1),
        ],
        axis=0,
    )
    coefficients = stacked(coefficients)
    loading = dot(coefficients, harm_high[...], ((1,), (0,)))
    loading = (
        loading[0:deep]
        + loading[deep : 2 * deep]
        + dot(coefficients[0:deep], harm_low[...], ((1,), (0,)))
    )

    pressure = fields[0] - loading
    east = fields[1]
    north = fields[2]
    step = fields[3]
    for _ in range(SUBSTEPS):
        east = east - steps[0] * (pltpu.roll(pressure, wide - 1, 1) - pressure)
        north = north - steps[1] * (pltpu.roll(pressure, tall - 1, 0) - pressure)
        pressure = pressure - step * (
            (east - pltpu.roll(east, 2, 1)) + (north - pltpu.roll(north, 2, 0))
        )
    east = pltpu.roll(east, 1, 1)
    north = pltpu.roll(north, 1, 0)
    surface = pressure + loading
    loading_out[...] = loading[0:rows, 0:cols]
    surface_out[...] = surface[0:rows, 0:cols]
    east_out_ref[...] = east[0:rows, 0:cols]
    north_out_ref[...] = north[0:rows, 0:cols]

    all_sent(0, a_in, n_lon - 1)
    all_sent(1, b_in, n_lat - 1)
    for copy in c_copies:
        copy.wait_send()
    pltpu.make_async_copy(packets(handed), packets(handed), d_send.at[n_z]).wait()
    pltpu.make_async_copy(packets(handed + 3), packets(handed + 3), d_send.at[far]).wait()
    left_copy.wait_send()
    right_copy.wait_send()

    @pl.when(lat > 0)
    def _():
        low_leg.wait_send()

    @pl.when(lat < n_lat - 1)
    def _():
        high_leg.wait_send()


def write_kernel(a_ref, b_ref, c_ref, d_ref, a_out, b_out, c_out, d_out, sem):
    pairs = ((a_ref, a_out), (b_ref, b_out), (c_ref, c_out), (d_ref, d_out))
    copies = [pltpu.make_async_copy(src, dst, sem.at[k]) for k, (src, dst) in enumerate(pairs)]
    for copy in copies:
        copy.start()
    for copy in copies:
        copy.wait()


def shards(height, east_flow, north_flow, legendre, love_numbers, wavenumbers, land_sea):
    n_lat, n_lon = lax.axis_size("lat"), lax.axis_size("lon")
    rows, cols = height.shape
    own, _, degrees = legendre.shape
    width = -(-(cols + 2 * HALO) // LANES) * LANES
    deep = rows + 2 * HALO
    chunk = degrees // (n_lat // 2)
    vmem = pl.BlockSpec(memory_space=pltpu.VMEM)
    f32 = jnp.float32
    shape = jax.ShapeDtypeStruct((rows, cols), f32)
    held = pltpu.VMEM((rows, cols), f32)
    results = pl.pallas_call(
        functools.partial(kernel, n_lat, n_lon),
        out_shape=(held, held, held, held),
        in_specs=[pl.BlockSpec(memory_space=pltpu.HBM)] * 7,
        out_specs=(vmem, vmem, vmem, vmem),
        scratch_shapes=[
            held,
            held,
            held,
            pltpu.VMEM((rows, cols), jnp.int32),
            pltpu.VMEM((1, degrees), f32),
            pltpu.VMEM((1, wavenumbers.shape[0]), jnp.int32),
            pltpu.VMEM((4, deep, width), f32),
            pltpu.VMEM((2, deep, width), f32),
            pltpu.VMEM((own * n_lon, LANES), f32),
            pltpu.VMEM((2 * own * n_lon, width), jnp.bfloat16),
            pltpu.VMEM((2 * own * n_lon, width), jnp.bfloat16),
            pltpu.VMEM((own, rows, degrees), f32),
            pltpu.VMEM((own * deep, degrees), jnp.bfloat16),
            pltpu.VMEM((own * deep, degrees), jnp.bfloat16),
            pltpu.VMEM((own, 2 * HALO, degrees), f32),
            pltpu.VMEM((n_lon, own, LANES), f32),
            pltpu.VMEM((n_lon, own, LANES), f32),
            pltpu.VMEM((n_lat // 2, 8, chunk), f32),
            pltpu.VMEM((n_lat, 8, chunk), f32),
            pltpu.VMEM((8, chunk), f32),
            pltpu.VMEM((n_lat // 2, 8, chunk), f32),
            pltpu.VMEM((5, LANES), f32),
            pltpu.VMEM((n_lon, 5, LANES), f32),
            pltpu.VMEM((deep, LANES), f32),
            pltpu.VMEM((deep, LANES), f32),
            pltpu.VMEM((deep, LANES), f32),
            pltpu.VMEM((deep, LANES), f32),
            pltpu.SemaphoreType.DMA((7,)),
            pltpu.SemaphoreType.DMA((2,)),
            pltpu.SemaphoreType.DMA((2,)),
            pltpu.SemaphoreType.DMA((6,)),
            pltpu.SemaphoreType.DMA((6,)),
            pltpu.SemaphoreType.DMA((n_lat // 2,)),
            pltpu.SemaphoreType.DMA((n_lat // 2,)),
            pltpu.SemaphoreType.DMA((n_lon // 4 + 1,)),
            pltpu.SemaphoreType.DMA((n_lon // 4 + 1,)),
        ],
        compiler_params=pltpu.CompilerParams(
            collective_id=0, has_side_effects=True, vmem_limit_bytes=24 << 20
        ),
    )(
        *[
            pltpu.with_memory_space_constraint(x, pltpu.HBM)
            for x in (
                height,
                east_flow,
                north_flow,
                land_sea,
                legendre,
                love_numbers.reshape(1, degrees),
                wavenumbers.reshape(1, wavenumbers.shape[0]),
            )
        ]
    )
    anywhere = pl.BlockSpec(memory_space=pl.ANY)
    return pl.pallas_call(
        write_kernel,
        out_shape=(shape, shape, shape, shape),
        in_specs=[vmem, vmem, vmem, vmem],
        out_specs=(anywhere, anywhere, anywhere, anywhere),
        scratch_shapes=[pltpu.SemaphoreType.DMA((4,))],
        compiler_params=pltpu.CompilerParams(vmem_limit_bytes=8 << 20),
    )(*results)


def solution(mesh):
    return jax.shard_map(
        shards,
        mesh=mesh,
        in_specs=(
            P("lat", "lon"),
            P("lat", "lon"),
            P("lat", "lon"),
            P("lon", "lat", None),
            P(),
            P(),
            P("lat", "lon"),
        ),
        out_specs=(P("lat", "lon"), P("lat", "lon"), P("lat", "lon"), P("lat", "lon")),
        check_vma=False,
    )
```

```python
import functools
import math

import jax
import jax.numpy as jnp
from jax import lax
from jax.experimental import pallas as pl
from jax.experimental.pallas import tpu as pltpu
from jax.sharding import PartitionSpec as P

SUBSTEPS = 4
HALO = 2 * SUBSTEPS
LANES = 128
STEP = 0.3
MESH = pl.DeviceIdType.MESH


def dot(a, b, dims):
    return lax.dot_general(a, b, (dims, ((), ())), preferred_element_type=jnp.float32)


def split(x):
    high = x.astype(jnp.bfloat16)
    return high, (x - high.astype(jnp.float32)).astype(jnp.bfloat16)


def stacked(x):
    return jnp.concatenate([x, x - x.astype(jnp.bfloat16).astype(jnp.float32)], axis=0).astype(
        jnp.bfloat16
    )


def hops(n, d):
    return min(d, n - d)


def lat_partners(n_lat, lat):
    n_y = n_lat // 2
    x_hi, y = lax.div(lat, n_y), lax.rem(lat, n_y)
    steps = [(2 * dx + hops(n_y, dy), dx, dy) for dx in range(2) for dy in range(n_y)]
    steps = sorted((step for step in steps if step[0]), reverse=True)
    return [
        (far, (1 - x_hi if dx else x_hi) * n_y + lax.rem(y + dy, n_y)) for far, dx, dy in steps
    ]


def lon_partners(n_lon, lon):
    n_z = n_lon // 4
    z, x_lo, core = lax.div(lon, 4), lax.rem(lax.div(lon, 2), 2), lax.rem(lon, 2)
    steps = [
        (hops(n_z, dz) + dx, dz, dx, dc)
        for dz in range(n_z)
        for dx in range(2)
        for dc in range(2)
        if dz or dx or dc
    ]
    return [
        (
            far,
            lax.rem(z + dz, n_z) * 4 + (1 - x_lo if dx else x_lo) * 2 + (1 - core if dc else core),
        )
        for far, dz, dx, dc in sorted(steps, reverse=True)
    ]


def kernel(
    n_lat,
    n_lon,
    height_hbm,
    east_hbm,
    north_hbm,
    land_hbm,
    legendre_ref,
    love_hbm,
    waves_hbm,
    loading_out,
    surface_out,
    east_out_ref,
    north_out_ref,
    height_ref,
    east_ref,
    north_ref,
    land_ref,
    love_ref,
    waves_ref,
    fields,
    steps,
    by_slot,
    harm_high,
    harm_low,
    leg_own,
    leg_high,
    leg_low,
    leg_halo,
    a_out,
    a_in,
    b_out,
    b_in,
    c_out,
    c_in,
    d_out,
    d_in,
    to_left,
    to_right,
    from_right,
    from_left,
    in_sem,
    send_sem,
    recv_sem,
    edge_send,
    edge_recv,
    c_send,
    c_recv,
):
    lat = lax.axis_index("lat")
    lon = lax.axis_index("lon")
    rows, cols = height_ref.shape
    own = legendre_ref.shape[0]
    width = fields.shape[2]
    period = cols * n_lon
    base, rest = cols // LANES * LANES, cols % LANES
    lats = lat_partners(n_lat, lat)
    lons = lon_partners(n_lon, lon)

    inputs = [
        pltpu.make_async_copy(src, dst, in_sem.at[k])
        for k, (src, dst) in enumerate(
            (
                (waves_hbm, waves_ref),
                (height_hbm, height_ref),
                (east_hbm, east_ref),
                (north_hbm, north_ref),
                (land_hbm, land_ref),
                (love_hbm, love_ref),
                (legendre_ref, leg_own),
            )
        )
    ]
    for copy in inputs:
        copy.start()
    barrier = pltpu.get_barrier_semaphore()
    everyone = [(far, (other, lon)) for far, other in lats]
    everyone += [(far, (lat, other)) for far, other in lons]
    for _, where in sorted(everyone, key=lambda other: -other[0]):
        pl.semaphore_signal(barrier, inc=1, device_id=where, device_id_type=MESH)
    n_y = n_lat // 2
    y = lax.rem(lat, n_y)
    for copy in inputs[:6]:
        copy.wait()

    for f, ref in enumerate((height_ref, east_ref, north_ref, land_ref)):
        fields[f, 0:rows, base:width] = jnp.zeros((rows, width - base), jnp.float32)
        fields[f, 0:rows, 0:cols] = ref[...].astype(jnp.float32)
    high, low = split(fields[0, 0:rows, :])
    twice_high = jnp.concatenate([high, high], axis=0)
    twice_low = jnp.concatenate([low, low], axis=0)

    count = waves_ref.shape[1]
    by_slot[...] = jnp.broadcast_to(waves_ref[...].astype(jnp.float32), (LANES, count)).T
    waves = jnp.concatenate([by_slot[pl.ds(m, n_lon, stride=own), :] for m in range(own)], axis=0)
    start = jnp.bitwise_and(waves.astype(jnp.int32) * lon, n_lon - 1).astype(jnp.float32) * cols
    quarter = period // 4
    lane = lax.broadcasted_iota(jnp.int32, (16, width), 1)
    column = jnp.where(lane < width - 64, lane, lane - width).astype(jnp.float32)
    for g in range(count // 16):
        here = slice(16 * g, 16 * g + 16)
        wave = jnp.concatenate([waves[here]] * (width // LANES), axis=1)
        first = jnp.concatenate([start[here]] * (width // LANES), axis=1)
        r = wave * column + first
        turn = (r * (1.0 / quarter) + 4096.5).astype(jnp.int32)
        d = r - (turn - 4096).astype(jnp.float32) * quarter
        phi = d * (2.0 * math.pi / period)
        s = phi * phi
        sin = 1.0 / 362880.0
        sin = sin * s - 1.0 / 5040.0
        sin = sin * s + 1.0 / 120.0
        sin = sin * s - 1.0 / 6.0
        sin = phi + phi * (s * sin)
        cos = -1.0 / 3628800.0
        cos = cos * s + 1.0 / 40320.0
        cos = cos * s - 1.0 / 720.0
        cos = cos * s + 1.0 / 24.0
        cos = cos * s - 0.5
        cos = 1.0 + s * cos
        odd = jnp.bitwise_and(turn, 1) == 1
        cos_minus = jnp.bitwise_and(turn + 1, 2) == 2
        sin_minus = jnp.bitwise_and(turn, 2) == 2
        c = jnp.where(odd, sin, cos)
        c = jnp.where(cos_minus, -c, c)
        n = jnp.where(odd, cos, sin)
        n = jnp.where(sin_minus, -n, n)
        there = slice(count + 16 * g, count + 16 * g + 16)
        harm_high[here, :], harm_low[here, :] = split(c)
        harm_high[there, :], harm_low[there, :] = split(n)

    partial = (
        dot(harm_high[...], twice_high, ((1,), (1,)))
        + dot(harm_high[...], twice_low, ((1,), (1,)))
        + dot(harm_low[...], twice_high, ((1,), (1,)))
    )
    half = lax.broadcasted_iota(jnp.int32, (count, LANES), 1) < rows
    partial = jnp.where(half, partial[0:count], partial[count : 2 * count])
    for m in range(own):
        a_out[:, m, :] = partial[n_lon * m : n_lon * (m + 1)]

    pl.semaphore_wait(barrier, n_lat + n_lon - 2)

    def lon_copy(k, src, dst, other):
        return pltpu.make_async_remote_copy(
            src_ref=src,
            dst_ref=dst,
            send_sem=send_sem.at[k],
            recv_sem=recv_sem.at[k],
            device_id=(lat, other),
            device_id_type=MESH,
        )

    def lat_copy(k, src, dst, other):
        return pltpu.make_async_remote_copy(
            src_ref=src,
            dst_ref=dst,
            send_sem=send_sem.at[k],
            recv_sem=recv_sem.at[k],
            device_id=(other, lon),
            device_id_type=MESH,
        )

    def all_received(k, ref, n):
        pltpu.make_async_copy(ref.at[pl.ds(0, n)], ref.at[pl.ds(0, n)], recv_sem.at[k]).wait()

    def all_sent(k, ref, n):
        pltpu.make_async_copy(ref.at[pl.ds(0, n)], ref.at[pl.ds(0, n)], send_sem.at[k]).wait()

    for _, other in lons:
        lon_copy(0, a_out.at[other], a_in.at[lon], other).start()
    a_in[lon] = a_out[lon]

    below, above = jnp.minimum(lat + 1, n_lat - 1), jnp.maximum(lat - 1, 0)

    def edge_copy(k, src, dst, where):
        return pltpu.make_async_remote_copy(
            src_ref=src,
            dst_ref=dst,
            send_sem=edge_send.at[k],
            recv_sem=edge_recv.at[k],
            device_id=where,
            device_id_type=MESH,
        )

    low_rows = edge_copy(
        0, fields.at[:, 0:HALO, :], fields.at[:, rows : rows + HALO, :], (above, lon)
    )
    high_rows = edge_copy(
        1,
        fields.at[:, rows - HALO : rows, :],
        fields.at[:, rows + HALO : rows + 2 * HALO, :],
        (below, lon),
    )
    halves = [pl.ds(0, own // 2), pl.ds(own // 2, own - own // 2)]
    low_leg = [
        edge_copy(
            k,
            legendre_ref.at[some, 0:HALO, :],
            leg_halo.at[some, 0:HALO, :],
            (above, lon),
        )
        for k, some in zip((2, 6), halves)
    ]
    high_leg = [
        edge_copy(
            k,
            legendre_ref.at[some, rows - HALO : rows, :],
            leg_halo.at[some, HALO : 2 * HALO, :],
            (below, lon),
        )
        for k, some in zip((3, 7), halves)
    ]

    @pl.when(lat > 0)
    def _():
        low_rows.start()
        low_leg[0].start()

    @pl.when(lat < n_lat - 1)
    def _():
        high_rows.start()
        high_leg[0].start()

    @pl.when(lat == 0)
    def _():
        fields[:, rows + HALO : rows + 2 * HALO, :] = jnp.zeros((4, HALO, width), jnp.float32)
        leg_halo[:, HALO : 2 * HALO, :] = jnp.zeros((own, HALO, leg_halo.shape[2]), jnp.float32)

    @pl.when(lat == n_lat - 1)
    def _():
        fields[:, rows : rows + HALO, :] = jnp.zeros((4, HALO, width), jnp.float32)
        leg_halo[:, 0:HALO, :] = jnp.zeros((own, HALO, leg_halo.shape[2]), jnp.float32)

    inputs[6].wait()
    inner_rows = own * rows
    for m in range(own):
        here = slice(rows * m, rows * (m + 1))
        leg_high[here, :], leg_low[here, :] = split(leg_own[m])
    all_received(0, a_in, n_lon - 1)
    fourier = jnp.sum(a_in[...], axis=0) * (1.0 / math.sqrt(period))

    degrees = leg_own.shape[2]
    lane8 = lax.broadcasted_iota(jnp.int32, (8, LANES), 1)
    row8 = lax.broadcasted_iota(jnp.int32, (8, LANES), 0)
    both = jnp.concatenate([fourier, fourier], axis=0)
    swapped = pltpu.roll(both, rows, 1)
    spread = jnp.where((lane8 < rows) == (row8 < 4), both, swapped)
    wave8 = jnp.bitwise_and(row8, 3)
    left = jnp.concatenate(
        [jnp.where(wave8 == 2 * h + lane8 // rows, spread, 0.0) for h in range(own * rows // LANES)],
        axis=1,
    )
    left = stacked(left)
    chunk = degrees // n_y
    bands = sorted(range(1, n_y), key=lambda dy: -hops(n_y, dy))
    for slot, dy in enumerate(bands + [0]):
        there = lax.rem(y + dy, n_y)
        block = pl.ds(pl.multiple_of(there * chunk, chunk), chunk)
        part = dot(left, leg_high[0:inner_rows, block], ((1,), (0,)))
        part = part[0:8] + part[8:16] + dot(left[0:8], leg_low[0:inner_rows, block], ((1,), (0,)))
        b_out[slot] = part
        lat_copy(1, b_out.at[slot], b_in.at[lat], n_lat - n_y - (lat - y) + there).start()
        if dy:
            lat_copy(1, b_out.at[slot], b_in.at[lat], lat - y + there).start()
        else:
            b_in[lat] = part

    @pl.when(lat > 0)
    def _():
        low_leg[1].start()

    @pl.when(lat < n_lat - 1)
    def _():
        high_leg[1].start()

    @pl.when(lat > 0)
    def _():
        high_rows.wait_recv()

    @pl.when(lat < n_lat - 1)
    def _():
        low_rows.wait_recv()

    deep = fields.shape[1]
    lane80 = lax.broadcasted_iota(jnp.int32, (deep, LANES), 1)
    packed_left = jnp.zeros((deep, LANES), jnp.float32)
    packed_right = jnp.zeros((deep, LANES), jnp.float32)
    for f in range(4):
        here = (lane80 >= 16 * f) & (lane80 < 16 * f + HALO)
        west = fields[f, :, 0:LANES]
        east = fields[f, :, base : base + LANES]
        packed_left = jnp.where(here, pltpu.roll(west, 16 * f, 1), packed_left)
        packed_right = jnp.where(
            here, pltpu.roll(east, (16 * f - (rest - HALO)) % LANES, 1), packed_right
        )
    to_left[...] = packed_left
    to_right[...] = packed_right
    west_side, east_side = lax.rem(lon + n_lon - 1, n_lon), lax.rem(lon + 1, n_lon)
    left_copy = edge_copy(4, to_left, from_right, (lat, west_side))
    right_copy = edge_copy(5, to_right, from_left, (lat, east_side))
    left_copy.start()
    right_copy.start()

    all_received(1, b_in, n_lat - 1)

    c_out[...] = jnp.sum(b_in[...], axis=0)
    c_copies = [
        pltpu.make_async_remote_copy(
            src_ref=c_out,
            dst_ref=c_in.at[y],
            send_sem=c_send.at[dy],
            recv_sem=c_recv.at[n_y - dy],
            device_id=(lat - y + lax.rem(y + dy, n_y), lon),
            device_id_type=MESH,
        )
        for dy in bands
    ]
    for copy in c_copies:
        copy.start()

    @pl.when(lat > 0)
    def _():
        low_rows.wait_send()

    @pl.when(lat < n_lat - 1)
    def _():
        high_rows.wait_send()

    left_copy.wait_recv()
    right_copy.wait_recv()
    right_halo = from_right[...]
    left_halo = from_left[...]
    for f in range(4):
        tile = fields[f, :, base : base + LANES]
        tile = jnp.where(
            (lane80 >= rest) & (lane80 < rest + HALO),
            pltpu.roll(right_halo, (rest - 16 * f) % LANES, 1),
            tile,
        )
        tile = jnp.where(
            lane80 >= LANES - HALO,
            pltpu.roll(left_halo, (LANES - HALO - 16 * f) % LANES, 1),
            tile,
        )
        fields[f, :, base : base + LANES] = tile

    @pl.when(lat > 0)
    def _():
        for copy in high_leg:
            copy.wait_recv()

    @pl.when(lat < n_lat - 1)
    def _():
        for copy in low_leg:
            copy.wait_recv()

    both_leg = split(leg_halo[...].reshape(own * 2 * HALO, degrees))
    leg_high[inner_rows:, :], leg_low[inner_rows:, :] = both_leg

    values = jnp.zeros((16, leg_high.shape[0]), jnp.float32)
    lows = jnp.zeros((8, leg_high.shape[0]), jnp.float32)
    for dy in [0] + bands[::-1]:
        there = lax.rem(y + dy, n_y)
        if dy:
            pltpu.make_async_copy(c_out, c_in.at[there], c_recv.at[dy]).wait()
        block = pl.ds(pl.multiple_of(there * chunk, chunk), chunk)
        spectral = stacked((c_in[there] if dy else c_out[...]) * love_ref[:, block])
        values = values + dot(spectral, leg_high[:, block], ((1,), (1,)))
        lows = lows + dot(spectral[0:8], leg_low[:, block], ((1,), (1,)))
    values = values[0:8] + values[8:16] + lows
    body = jnp.zeros((8, LANES), jnp.float32)
    for h in range(inner_rows // LANES):
        body = body + jnp.where(
            wave8 == 2 * h + lane8 // rows, values[:, LANES * h : LANES * (h + 1)], 0.0
        )
    body = body + pltpu.roll(body, rows, 1)
    body = jnp.where(lane8 < rows, body, pltpu.roll(body, 4, 0))
    rim = jnp.concatenate(
        [values[:, inner_rows:], jnp.zeros((8, LANES - own * 2 * HALO), jnp.float32)], axis=1
    )
    rim = jnp.where(wave8 == lane8 // (2 * HALO), rim, 0.0)
    rim = jnp.where(row8 < 4, rim, pltpu.roll(rim, own * 2 * HALO, 1))
    rim = jnp.sum(rim, axis=0, keepdims=True)
    packet = jnp.where(row8 < 4, body, rim) * (1.0 / math.sqrt(count))
    d_out[...] = packet[0:5]
    for _, other in lons:
        lon_copy(3, d_out, d_in.at[lon], other).start()
    d_in[lon] = d_out[...]

    wide, tall = width - 1, deep - 1
    wet = fields[3]
    step = wet * STEP
    fields[1] = pltpu.roll(fields[1] * wet, wide, 1)
    fields[2] = pltpu.roll(fields[2] * wet, tall, 0)
    fields[3] = step
    steps[0] = pltpu.roll(step, wide, 1)
    steps[1] = pltpu.roll(step, tall, 0)
    all_received(3, d_in, n_lon - 1)

    rows_kt = jnp.concatenate([d_in[:, m, :] for m in range(own)], axis=0)
    rows_tk = rows_kt.T
    rim_kt = jnp.concatenate(
        [d_in[:, 4, :], jnp.zeros((count - n_lon, LANES), jnp.float32)], axis=0
    )
    rim_tk = rim_kt.T
    rims = []
    for p in range(2):
        side = rim_tk[2 * HALO * own * p : 2 * HALO * (own * p + 1)]
        for m in range(1, own):
            first = 2 * HALO * (own * p + m)
            side = side + pltpu.roll(rim_tk[first : first + 2 * HALO], n_lon * m, 1)
        rims.append(side)
    coefficients = jnp.concatenate(
        [
            jnp.concatenate([rows_tk[0:rows], rows_tk[rows : 2 * rows]], axis=1),
            jnp.concatenate(rims, axis=1),
        ],
        axis=0,
    )
    coefficients = stacked(coefficients)
    loading = dot(coefficients, harm_high[...], ((1,), (0,)))
    loading = (
        loading[0:deep]
        + loading[deep : 2 * deep]
        + dot(coefficients[0:deep], harm_low[...], ((1,), (0,)))
    )

    pressure = fields[0] - loading
    east = fields[1]
    north = fields[2]
    step = fields[3]
    for _ in range(SUBSTEPS):
        east = east - steps[0] * (pltpu.roll(pressure, wide - 1, 1) - pressure)
        north = north - steps[1] * (pltpu.roll(pressure, tall - 1, 0) - pressure)
        pressure = pressure - step * (
            (east - pltpu.roll(east, 2, 1)) + (north - pltpu.roll(north, 2, 0))
        )
    east = pltpu.roll(east, 1, 1)
    north = pltpu.roll(north, 1, 0)
    surface = pressure + loading
    loading_out[...] = loading[0:rows, 0:cols]
    surface_out[...] = surface[0:rows, 0:cols]
    east_out_ref[...] = east[0:rows, 0:cols]
    north_out_ref[...] = north[0:rows, 0:cols]

    all_sent(0, a_in, n_lon - 1)
    all_sent(1, b_in, n_lat - 1)
    for copy in c_copies:
        copy.wait_send()
    all_sent(3, d_in, n_lon - 1)
    left_copy.wait_send()
    right_copy.wait_send()

    @pl.when(lat > 0)
    def _():
        for copy in low_leg:
            copy.wait_send()

    @pl.when(lat < n_lat - 1)
    def _():
        for copy in high_leg:
            copy.wait_send()


def write_kernel(a_ref, b_ref, c_ref, d_ref, a_out, b_out, c_out, d_out, sem):
    pairs = ((a_ref, a_out), (b_ref, b_out), (c_ref, c_out), (d_ref, d_out))
    copies = [pltpu.make_async_copy(src, dst, sem.at[k]) for k, (src, dst) in enumerate(pairs)]
    for copy in copies:
        copy.start()
    for copy in copies:
        copy.wait()


def shards(height, east_flow, north_flow, legendre, love_numbers, wavenumbers, land_sea):
    n_lat, n_lon = lax.axis_size("lat"), lax.axis_size("lon")
    rows, cols = height.shape
    own, _, degrees = legendre.shape
    width = -(-(cols + 2 * HALO) // LANES) * LANES
    deep = rows + 2 * HALO
    chunk = degrees // (n_lat // 2)
    vmem = pl.BlockSpec(memory_space=pltpu.VMEM)
    f32 = jnp.float32
    shape = jax.ShapeDtypeStruct((rows, cols), f32)
    held = pltpu.VMEM((rows, cols), f32)
    results = pl.pallas_call(
        functools.partial(kernel, n_lat, n_lon),
        out_shape=(held, held, held, held),
        in_specs=[pl.BlockSpec(memory_space=pltpu.HBM)] * 7,
        out_specs=(vmem, vmem, vmem, vmem),
        scratch_shapes=[
            held,
            held,
            held,
            pltpu.VMEM((rows, cols), jnp.int32),
            pltpu.VMEM((1, degrees), f32),
            pltpu.VMEM((1, wavenumbers.shape[0]), jnp.int32),
            pltpu.VMEM((4, deep, width), f32),
            pltpu.VMEM((2, deep, width), f32),
            pltpu.VMEM((own * n_lon, LANES), f32),
            pltpu.VMEM((2 * own * n_lon, width), jnp.bfloat16),
            pltpu.VMEM((2 * own * n_lon, width), jnp.bfloat16),
            pltpu.VMEM((own, rows, degrees), f32),
            pltpu.VMEM((own * deep, degrees), jnp.bfloat16),
            pltpu.VMEM((own * deep, degrees), jnp.bfloat16),
            pltpu.VMEM((own, 2 * HALO, degrees), f32),
            pltpu.VMEM((n_lon, own, LANES), f32),
            pltpu.VMEM((n_lon, own, LANES), f32),
            pltpu.VMEM((n_lat // 2, 8, chunk), f32),
            pltpu.VMEM((n_lat, 8, chunk), f32),
            pltpu.VMEM((8, chunk), f32),
            pltpu.VMEM((n_lat // 2, 8, chunk), f32),
            pltpu.VMEM((5, LANES), f32),
            pltpu.VMEM((n_lon, 5, LANES), f32),
            pltpu.VMEM((deep, LANES), f32),
            pltpu.VMEM((deep, LANES), f32),
            pltpu.VMEM((deep, LANES), f32),
            pltpu.VMEM((deep, LANES), f32),
            pltpu.SemaphoreType.DMA((7,)),
            pltpu.SemaphoreType.DMA((4,)),
            pltpu.SemaphoreType.DMA((4,)),
            pltpu.SemaphoreType.DMA((8,)),
            pltpu.SemaphoreType.DMA((8,)),
            pltpu.SemaphoreType.DMA((n_lat // 2,)),
            pltpu.SemaphoreType.DMA((n_lat // 2,)),
        ],
        compiler_params=pltpu.CompilerParams(
            collective_id=0, has_side_effects=True, vmem_limit_bytes=24 << 20
        ),
    )(
        *[
            pltpu.with_memory_space_constraint(x, pltpu.HBM)
            for x in (
                height,
                east_flow,
                north_flow,
                land_sea,
                legendre,
                love_numbers.reshape(1, degrees),
                wavenumbers.reshape(1, wavenumbers.shape[0]),
            )
        ]
    )
    anywhere = pl.BlockSpec(memory_space=pl.ANY)
    return pl.pallas_call(
        write_kernel,
        out_shape=(shape, shape, shape, shape),
        in_specs=[vmem, vmem, vmem, vmem],
        out_specs=(anywhere, anywhere, anywhere, anywhere),
        scratch_shapes=[pltpu.SemaphoreType.DMA((4,))],
        compiler_params=pltpu.CompilerParams(vmem_limit_bytes=8 << 20),
    )(*results)


def solution(mesh):
    return jax.shard_map(
        shards,
        mesh=mesh,
        in_specs=(
            P("lat", "lon"),
            P("lat", "lon"),
            P("lat", "lon"),
            P("lon", "lat", None),
            P(),
            P(),
            P("lat", "lon"),
        ),
        out_specs=(P("lat", "lon"), P("lat", "lon"), P("lat", "lon"), P("lat", "lon")),
        check_vma=False,
    )
```

```python
import functools
import math

import jax
import jax.numpy as jnp
from jax import lax
from jax.experimental import pallas as pl
from jax.experimental.pallas import tpu as pltpu
from jax.sharding import PartitionSpec as P

SUBSTEPS = 4
HALO = 2 * SUBSTEPS
LANES = 128
STEP = 0.3
MESH = pl.DeviceIdType.MESH


def dot(a, b, dims):
    return lax.dot_general(a, b, (dims, ((), ())), preferred_element_type=jnp.float32)


def split(x):
    high = x.astype(jnp.bfloat16)
    return high, (x - high.astype(jnp.float32)).astype(jnp.bfloat16)


def stacked(x):
    return jnp.concatenate([x, x - x.astype(jnp.bfloat16).astype(jnp.float32)], axis=0).astype(
        jnp.bfloat16
    )


def hops(n, d):
    return min(d, n - d)


def lat_partners(n_lat, lat):
    n_y = n_lat // 2
    x_hi, y = lax.div(lat, n_y), lax.rem(lat, n_y)
    steps = [(2 * dx + hops(n_y, dy), dx, dy) for dx in range(2) for dy in range(n_y)]
    steps = sorted((step for step in steps if step[0]), reverse=True)
    return [
        (far, (1 - x_hi if dx else x_hi) * n_y + lax.rem(y + dy, n_y)) for far, dx, dy in steps
    ]


def lon_partners(n_lon, lon):
    n_z = n_lon // 4
    z, x_lo, core = lax.div(lon, 4), lax.rem(lax.div(lon, 2), 2), lax.rem(lon, 2)
    steps = [
        (hops(n_z, dz) + dx, dz, dx, dc)
        for dz in range(n_z)
        for dx in range(2)
        for dc in range(2)
        if dz or dx or dc
    ]
    return [
        (
            far,
            lax.rem(z + dz, n_z) * 4 + (1 - x_lo if dx else x_lo) * 2 + (1 - core if dc else core),
        )
        for far, dz, dx, dc in sorted(steps, reverse=True)
    ]


def kernel(
    n_lat,
    n_lon,
    height_hbm,
    east_hbm,
    north_hbm,
    land_hbm,
    legendre_ref,
    love_hbm,
    waves_hbm,
    loading_out,
    surface_out,
    east_out_ref,
    north_out_ref,
    height_ref,
    east_ref,
    north_ref,
    land_ref,
    love_ref,
    waves_ref,
    fields,
    steps,
    by_slot,
    harm_high,
    harm_low,
    leg_own,
    leg_high,
    leg_low,
    leg_halo,
    a_out,
    a_in,
    b_out,
    b_in,
    c_out,
    c_in,
    d_out,
    d_in,
    to_left,
    to_right,
    from_right,
    from_left,
    in_sem,
    send_sem,
    recv_sem,
    edge_send,
    edge_recv,
    c_send,
    c_recv,
):
    lat = lax.axis_index("lat")
    lon = lax.axis_index("lon")
    rows, cols = height_ref.shape
    own = legendre_ref.shape[0]
    width = fields.shape[2]
    period = cols * n_lon
    base, rest = cols // LANES * LANES, cols % LANES
    lats = lat_partners(n_lat, lat)
    lons = lon_partners(n_lon, lon)

    inputs = [
        pltpu.make_async_copy(src, dst, in_sem.at[k])
        for k, (src, dst) in enumerate(
            (
                (waves_hbm, waves_ref),
                (height_hbm, height_ref),
                (east_hbm, east_ref),
                (north_hbm, north_ref),
                (land_hbm, land_ref),
                (love_hbm, love_ref),
                (legendre_ref, leg_own),
            )
        )
    ]
    for copy in inputs:
        copy.start()
    barrier = pltpu.get_barrier_semaphore()
    everyone = [(far, (other, lon)) for far, other in lats]
    everyone += [(far, (lat, other)) for far, other in lons]
    for _, where in sorted(everyone, key=lambda other: -other[0]):
        pl.semaphore_signal(barrier, inc=1, device_id=where, device_id_type=MESH)
    n_y = n_lat // 2
    y = lax.rem(lat, n_y)
    for copy in inputs[:6]:
        copy.wait()

    for f, ref in enumerate((height_ref, east_ref, north_ref, land_ref)):
        fields[f, 0:rows, base:width] = jnp.zeros((rows, width - base), jnp.float32)
        fields[f, 0:rows, 0:cols] = ref[...].astype(jnp.float32)
    high, low = split(fields[0, 0:rows, :])
    twice_high = jnp.concatenate([high, high], axis=0)
    twice_low = jnp.concatenate([low, low], axis=0)

    count = waves_ref.shape[1]
    by_slot[...] = jnp.broadcast_to(waves_ref[...].astype(jnp.float32), (LANES, count)).T
    waves = jnp.concatenate([by_slot[pl.ds(m, n_lon, stride=own), :] for m in range(own)], axis=0)
    start = jnp.bitwise_and(waves.astype(jnp.int32) * lon, n_lon - 1).astype(jnp.float32) * cols
    quarter = period // 4
    lane = lax.broadcasted_iota(jnp.int32, (16, width), 1)
    column = jnp.where(lane < width - 64, lane, lane - width).astype(jnp.float32)
    for g in range(count // 16):
        here = slice(16 * g, 16 * g + 16)
        wave = jnp.concatenate([waves[here]] * (width // LANES), axis=1)
        first = jnp.concatenate([start[here]] * (width // LANES), axis=1)
        r = wave * column + first
        turn = (r * (1.0 / quarter) + 4096.5).astype(jnp.int32)
        d = r - (turn - 4096).astype(jnp.float32) * quarter
        phi = d * (2.0 * math.pi / period)
        s = phi * phi
        sin = 1.0 / 362880.0
        sin = sin * s - 1.0 / 5040.0
        sin = sin * s + 1.0 / 120.0
        sin = sin * s - 1.0 / 6.0
        sin = phi + phi * (s * sin)
        cos = -1.0 / 3628800.0
        cos = cos * s + 1.0 / 40320.0
        cos = cos * s - 1.0 / 720.0
        cos = cos * s + 1.0 / 24.0
        cos = cos * s - 0.5
        cos = 1.0 + s * cos
        odd = jnp.bitwise_and(turn, 1) == 1
        cos_minus = jnp.bitwise_and(turn + 1, 2) == 2
        sin_minus = jnp.bitwise_and(turn, 2) == 2
        c = jnp.where(odd, sin, cos)
        c = jnp.where(cos_minus, -c, c)
        n = jnp.where(odd, cos, sin)
        n = jnp.where(sin_minus, -n, n)
        there = slice(count + 16 * g, count + 16 * g + 16)
        harm_high[here, :], harm_low[here, :] = split(c)
        harm_high[there, :], harm_low[there, :] = split(n)

    partial = (
        dot(harm_high[...], twice_high, ((1,), (1,)))
        + dot(harm_high[...], twice_low, ((1,), (1,)))
        + dot(harm_low[...], twice_high, ((1,), (1,)))
    )
    half = lax.broadcasted_iota(jnp.int32, (count, LANES), 1) < rows
    partial = jnp.where(half, partial[0:count], partial[count : 2 * count])
    for m in range(own):
        a_out[:, m, :] = partial[n_lon * m : n_lon * (m + 1)]

    pl.semaphore_wait(barrier, n_lat + n_lon - 2)

    def lon_copy(k, src, dst, other):
        return pltpu.make_async_remote_copy(
            src_ref=src,
            dst_ref=dst,
            send_sem=send_sem.at[k],
            recv_sem=recv_sem.at[k],
            device_id=(lat, other),
            device_id_type=MESH,
        )

    def lat_copy(k, src, dst, other):
        return pltpu.make_async_remote_copy(
            src_ref=src,
            dst_ref=dst,
            send_sem=send_sem.at[k],
            recv_sem=recv_sem.at[k],
            device_id=(other, lon),
            device_id_type=MESH,
        )

    def all_received(k, ref, n):
        pltpu.make_async_copy(ref.at[pl.ds(0, n)], ref.at[pl.ds(0, n)], recv_sem.at[k]).wait()

    def all_sent(k, ref, n):
        pltpu.make_async_copy(ref.at[pl.ds(0, n)], ref.at[pl.ds(0, n)], send_sem.at[k]).wait()

    for _, other in lons:
        lon_copy(0, a_out.at[other], a_in.at[lon], other).start()
    a_in[lon] = a_out[lon]

    below, above = jnp.minimum(lat + 1, n_lat - 1), jnp.maximum(lat - 1, 0)

    def edge_copy(k, src, dst, where):
        return pltpu.make_async_remote_copy(
            src_ref=src,
            dst_ref=dst,
            send_sem=edge_send.at[k],
            recv_sem=edge_recv.at[k],
            device_id=where,
            device_id_type=MESH,
        )

    low_rows = edge_copy(
        0, fields.at[:, 0:HALO, :], fields.at[:, rows : rows + HALO, :], (above, lon)
    )
    high_rows = edge_copy(
        1,
        fields.at[:, rows - HALO : rows, :],
        fields.at[:, rows + HALO : rows + 2 * HALO, :],
        (below, lon),
    )
    halves = [pl.ds(0, own // 4), pl.ds(own // 4, own - own // 4)]
    low_leg = [
        edge_copy(
            k,
            legendre_ref.at[some, 0:HALO, :],
            leg_halo.at[some, 0:HALO, :],
            (above, lon),
        )
        for k, some in zip((2, 6), halves)
    ]
    high_leg = [
        edge_copy(
            k,
            legendre_ref.at[some, rows - HALO : rows, :],
            leg_halo.at[some, HALO : 2 * HALO, :],
            (below, lon),
        )
        for k, some in zip((3, 7), halves)
    ]

    @pl.when(lat > 0)
    def _():
        low_rows.start()
        low_leg[0].start()

    @pl.when(lat < n_lat - 1)
    def _():
        high_rows.start()
        high_leg[0].start()

    @pl.when(lat == 0)
    def _():
        fields[:, rows + HALO : rows + 2 * HALO, :] = jnp.zeros((4, HALO, width), jnp.float32)
        leg_halo[:, HALO : 2 * HALO, :] = jnp.zeros((own, HALO, leg_halo.shape[2]), jnp.float32)

    @pl.when(lat == n_lat - 1)
    def _():
        fields[:, rows : rows + HALO, :] = jnp.zeros((4, HALO, width), jnp.float32)
        leg_halo[:, 0:HALO, :] = jnp.zeros((own, HALO, leg_halo.shape[2]), jnp.float32)

    inputs[6].wait()
    inner_rows = own * rows
    for m in range(own):
        here = slice(rows * m, rows * (m + 1))
        leg_high[here, :], leg_low[here, :] = split(leg_own[m])
    all_received(0, a_in, n_lon - 1)
    fourier = jnp.sum(a_in[...], axis=0) * (1.0 / math.sqrt(period))

    degrees = leg_own.shape[2]
    lane8 = lax.broadcasted_iota(jnp.int32, (8, LANES), 1)
    row8 = lax.broadcasted_iota(jnp.int32, (8, LANES), 0)
    both = jnp.concatenate([fourier, fourier], axis=0)
    swapped = pltpu.roll(both, rows, 1)
    spread = jnp.where((lane8 < rows) == (row8 < 4), both, swapped)
    wave8 = jnp.bitwise_and(row8, 3)
    left = jnp.concatenate(
        [jnp.where(wave8 == 2 * h + lane8 // rows, spread, 0.0) for h in range(own * rows // LANES)],
        axis=1,
    )
    left = stacked(left)
    chunk = degrees // n_y
    bands = sorted(range(1, n_y), key=lambda dy: -hops(n_y, dy))
    for slot, dy in enumerate(bands + [0]):
        there = lax.rem(y + dy, n_y)
        block = pl.ds(pl.multiple_of(there * chunk, chunk), chunk)
        part = dot(left, leg_high[0:inner_rows, block], ((1,), (0,)))
        part = part[0:8] + part[8:16] + dot(left[0:8], leg_low[0:inner_rows, block], ((1,), (0,)))
        b_out[slot] = part
        lat_copy(1, b_out.at[slot], b_in.at[lat], n_lat - n_y - (lat - y) + there).start()
        if dy:
            lat_copy(1, b_out.at[slot], b_in.at[lat], lat - y + there).start()
        else:
            b_in[lat] = part

    @pl.when(lat > 0)
    def _():
        low_leg[1].start()

    @pl.when(lat < n_lat - 1)
    def _():
        high_leg[1].start()

    @pl.when(lat > 0)
    def _():
        high_rows.wait_recv()

    @pl.when(lat < n_lat - 1)
    def _():
        low_rows.wait_recv()

    deep = fields.shape[1]
    lane80 = lax.broadcasted_iota(jnp.int32, (deep, LANES), 1)
    packed_left = jnp.zeros((deep, LANES), jnp.float32)
    packed_right = jnp.zeros((deep, LANES), jnp.float32)
    for f in range(4):
        here = (lane80 >= 16 * f) & (lane80 < 16 * f + HALO)
        west = fields[f, :, 0:LANES]
        east = fields[f, :, base : base + LANES]
        packed_left = jnp.where(here, pltpu.roll(west, 16 * f, 1), packed_left)
        packed_right = jnp.where(
            here, pltpu.roll(east, (16 * f - (rest - HALO)) % LANES, 1), packed_right
        )
    to_left[...] = packed_left
    to_right[...] = packed_right
    west_side, east_side = lax.rem(lon + n_lon - 1, n_lon), lax.rem(lon + 1, n_lon)
    left_copy = edge_copy(4, to_left, from_right, (lat, west_side))
    right_copy = edge_copy(5, to_right, from_left, (lat, east_side))
    left_copy.start()
    right_copy.start()

    all_received(1, b_in, n_lat - 1)

    c_out[...] = jnp.sum(b_in[...], axis=0)
    c_copies = [
        pltpu.make_async_remote_copy(
            src_ref=c_out,
            dst_ref=c_in.at[y],
            send_sem=c_send.at[dy],
            recv_sem=c_recv.at[n_y - dy],
            device_id=(lat - y + lax.rem(y + dy, n_y), lon),
            device_id_type=MESH,
        )
        for dy in bands
    ]
    for copy in c_copies:
        copy.start()

    @pl.when(lat > 0)
    def _():
        low_rows.wait_send()

    @pl.when(lat < n_lat - 1)
    def _():
        high_rows.wait_send()

    left_copy.wait_recv()
    right_copy.wait_recv()
    right_halo = from_right[...]
    left_halo = from_left[...]
    for f in range(4):
        tile = fields[f, :, base : base + LANES]
        tile = jnp.where(
            (lane80 >= rest) & (lane80 < rest + HALO),
            pltpu.roll(right_halo, (rest - 16 * f) % LANES, 1),
            tile,
        )
        tile = jnp.where(
            lane80 >= LANES - HALO,
            pltpu.roll(left_halo, (LANES - HALO - 16 * f) % LANES, 1),
            tile,
        )
        fields[f, :, base : base + LANES] = tile

    @pl.when(lat > 0)
    def _():
        for copy in high_leg:
            copy.wait_recv()

    @pl.when(lat < n_lat - 1)
    def _():
        for copy in low_leg:
            copy.wait_recv()

    both_leg = split(leg_halo[...].reshape(own * 2 * HALO, degrees))
    leg_high[inner_rows:, :], leg_low[inner_rows:, :] = both_leg

    values = jnp.zeros((16, leg_high.shape[0]), jnp.float32)
    lows = jnp.zeros((8, leg_high.shape[0]), jnp.float32)
    for dy in [0] + bands[::-1]:
        there = lax.rem(y + dy, n_y)
        if dy:
            pltpu.make_async_copy(c_out, c_in.at[there], c_recv.at[dy]).wait()
        block = pl.ds(pl.multiple_of(there * chunk, chunk), chunk)
        spectral = stacked((c_in[there] if dy else c_out[...]) * love_ref[:, block])
        values = values + dot(spectral, leg_high[:, block], ((1,), (1,)))
        lows = lows + dot(spectral[0:8], leg_low[:, block], ((1,), (1,)))
    values = values[0:8] + values[8:16] + lows
    body = jnp.zeros((8, LANES), jnp.float32)
    for h in range(inner_rows // LANES):
        body = body + jnp.where(
            wave8 == 2 * h + lane8 // rows, values[:, LANES * h : LANES * (h + 1)], 0.0
        )
    body = body + pltpu.roll(body, rows, 1)
    body = jnp.where(lane8 < rows, body, pltpu.roll(body, 4, 0))
    rim = jnp.concatenate(
        [values[:, inner_rows:], jnp.zeros((8, LANES - own * 2 * HALO), jnp.float32)], axis=1
    )
    rim = jnp.where(wave8 == lane8 // (2 * HALO), rim, 0.0)
    rim = jnp.where(row8 < 4, rim, pltpu.roll(rim, own * 2 * HALO, 1))
    rim = jnp.sum(rim, axis=0, keepdims=True)
    packet = jnp.where(row8 < 4, body, rim) * (1.0 / math.sqrt(count))
    d_out[...] = packet[0:5]
    for _, other in lons:
        lon_copy(3, d_out, d_in.at[lon], other).start()
    d_in[lon] = d_out[...]

    wide, tall = width - 1, deep - 1
    wet = fields[3]
    step = wet * STEP
    fields[1] = pltpu.roll(fields[1] * wet, wide, 1)
    fields[2] = pltpu.roll(fields[2] * wet, tall, 0)
    fields[3] = step
    steps[0] = pltpu.roll(step, wide, 1)
    steps[1] = pltpu.roll(step, tall, 0)
    all_received(3, d_in, n_lon - 1)

    rows_kt = jnp.concatenate([d_in[:, m, :] for m in range(own)], axis=0)
    rows_tk = rows_kt.T
    rim_kt = jnp.concatenate(
        [d_in[:, 4, :], jnp.zeros((count - n_lon, LANES), jnp.float32)], axis=0
    )
    rim_tk = rim_kt.T
    rims = []
    for p in range(2):
        side = rim_tk[2 * HALO * own * p : 2 * HALO * (own * p + 1)]
        for m in range(1, own):
            first = 2 * HALO * (own * p + m)
            side = side + pltpu.roll(rim_tk[first : first + 2 * HALO], n_lon * m, 1)
        rims.append(side)
    coefficients = jnp.concatenate(
        [
            jnp.concatenate([rows_tk[0:rows], rows_tk[rows : 2 * rows]], axis=1),
            jnp.concatenate(rims, axis=1),
        ],
        axis=0,
    )
    coefficients = stacked(coefficients)
    loading = dot(coefficients, harm_high[...], ((1,), (0,)))
    loading = (
        loading[0:deep]
        + loading[deep : 2 * deep]
        + dot(coefficients[0:deep], harm_low[...], ((1,), (0,)))
    )

    pressure = fields[0] - loading
    east = fields[1]
    north = fields[2]
    step = fields[3]
    for _ in range(SUBSTEPS):
        east = east - steps[0] * (pltpu.roll(pressure, wide - 1, 1) - pressure)
        north = north - steps[1] * (pltpu.roll(pressure, tall - 1, 0) - pressure)
        pressure = pressure - step * (
            (east - pltpu.roll(east, 2, 1)) + (north - pltpu.roll(north, 2, 0))
        )
    east = pltpu.roll(east, 1, 1)
    north = pltpu.roll(north, 1, 0)
    surface = pressure + loading
    loading_out[...] = loading[0:rows, 0:cols]
    surface_out[...] = surface[0:rows, 0:cols]
    east_out_ref[...] = east[0:rows, 0:cols]
    north_out_ref[...] = north[0:rows, 0:cols]

    all_sent(0, a_in, n_lon - 1)
    all_sent(1, b_in, n_lat - 1)
    for copy in c_copies:
        copy.wait_send()
    all_sent(3, d_in, n_lon - 1)
    left_copy.wait_send()
    right_copy.wait_send()

    @pl.when(lat > 0)
    def _():
        for copy in low_leg:
            copy.wait_send()

    @pl.when(lat < n_lat - 1)
    def _():
        for copy in high_leg:
            copy.wait_send()


def write_kernel(a_ref, b_ref, c_ref, d_ref, a_out, b_out, c_out, d_out, sem):
    pairs = ((a_ref, a_out), (b_ref, b_out), (c_ref, c_out), (d_ref, d_out))
    copies = [pltpu.make_async_copy(src, dst, sem.at[k]) for k, (src, dst) in enumerate(pairs)]
    for copy in copies:
        copy.start()
    for copy in copies:
        copy.wait()


def shards(height, east_flow, north_flow, legendre, love_numbers, wavenumbers, land_sea):
    n_lat, n_lon = lax.axis_size("lat"), lax.axis_size("lon")
    rows, cols = height.shape
    own, _, degrees = legendre.shape
    width = -(-(cols + 2 * HALO) // LANES) * LANES
    deep = rows + 2 * HALO
    chunk = degrees // (n_lat // 2)
    vmem = pl.BlockSpec(memory_space=pltpu.VMEM)
    f32 = jnp.float32
    shape = jax.ShapeDtypeStruct((rows, cols), f32)
    held = pltpu.VMEM((rows, cols), f32)
    results = pl.pallas_call(
        functools.partial(kernel, n_lat, n_lon),
        out_shape=(held, held, held, held),
        in_specs=[pl.BlockSpec(memory_space=pltpu.HBM)] * 7,
        out_specs=(vmem, vmem, vmem, vmem),
        scratch_shapes=[
            held,
            held,
            held,
            pltpu.VMEM((rows, cols), jnp.int32),
            pltpu.VMEM((1, degrees), f32),
            pltpu.VMEM((1, wavenumbers.shape[0]), jnp.int32),
            pltpu.VMEM((4, deep, width), f32),
            pltpu.VMEM((2, deep, width), f32),
            pltpu.VMEM((own * n_lon, LANES), f32),
            pltpu.VMEM((2 * own * n_lon, width), jnp.bfloat16),
            pltpu.VMEM((2 * own * n_lon, width), jnp.bfloat16),
            pltpu.VMEM((own, rows, degrees), f32),
            pltpu.VMEM((own * deep, degrees), jnp.bfloat16),
            pltpu.VMEM((own * deep, degrees), jnp.bfloat16),
            pltpu.VMEM((own, 2 * HALO, degrees), f32),
            pltpu.VMEM((n_lon, own, LANES), f32),
            pltpu.VMEM((n_lon, own, LANES), f32),
            pltpu.VMEM((n_lat // 2, 8, chunk), f32),
            pltpu.VMEM((n_lat, 8, chunk), f32),
            pltpu.VMEM((8, chunk), f32),
            pltpu.VMEM((n_lat // 2, 8, chunk), f32),
            pltpu.VMEM((5, LANES), f32),
            pltpu.VMEM((n_lon, 5, LANES), f32),
            pltpu.VMEM((deep, LANES), f32),
            pltpu.VMEM((deep, LANES), f32),
            pltpu.VMEM((deep, LANES), f32),
            pltpu.VMEM((deep, LANES), f32),
            pltpu.SemaphoreType.DMA((7,)),
            pltpu.SemaphoreType.DMA((4,)),
            pltpu.SemaphoreType.DMA((4,)),
            pltpu.SemaphoreType.DMA((8,)),
            pltpu.SemaphoreType.DMA((8,)),
            pltpu.SemaphoreType.DMA((n_lat // 2,)),
            pltpu.SemaphoreType.DMA((n_lat // 2,)),
        ],
        compiler_params=pltpu.CompilerParams(
            collective_id=0, has_side_effects=True, vmem_limit_bytes=24 << 20
        ),
    )(
        *[
            pltpu.with_memory_space_constraint(x, pltpu.HBM)
            for x in (
                height,
                east_flow,
                north_flow,
                land_sea,
                legendre,
                love_numbers.reshape(1, degrees),
                wavenumbers.reshape(1, wavenumbers.shape[0]),
            )
        ]
    )
    anywhere = pl.BlockSpec(memory_space=pl.ANY)
    return pl.pallas_call(
        write_kernel,
        out_shape=(shape, shape, shape, shape),
        in_specs=[vmem, vmem, vmem, vmem],
        out_specs=(anywhere, anywhere, anywhere, anywhere),
        scratch_shapes=[pltpu.SemaphoreType.DMA((4,))],
        compiler_params=pltpu.CompilerParams(vmem_limit_bytes=8 << 20),
    )(*results)


def solution(mesh):
    return jax.shard_map(
        shards,
        mesh=mesh,
        in_specs=(
            P("lat", "lon"),
            P("lat", "lon"),
            P("lat", "lon"),
            P("lon", "lat", None),
            P(),
            P(),
            P("lat", "lon"),
        ),
        out_specs=(P("lat", "lon"), P("lat", "lon"), P("lat", "lon"), P("lat", "lon")),
        check_vma=False,
    )
```
